512 devices in a mesh: seq: 64 (over z_hi, x, y), tp: 8 (over z_lo, core).
Axes of the slice: x: 4, y: 8, z: 8 (z_hi: 2, z_lo: 4; z = z_hi * 4 + z_lo), core: 2. Of those that a mesh axis runs over, the one named last changes fastest.
Arguments:
- features: bfloat16 [8192, 8192], P('seq', 'tp'), may hold values from -6 to 6
- in_proj: bfloat16 [3, 8192, 1024], P(None, 'seq', 'tp'), may hold values from -0.0625 to 0.0625
- short_taps: float32 [3, 3, 1024], P(None, None, 'tp'), may hold values from -3 to 3
- long_filter: float32 [8192, 1024], P('seq', 'tp'), may hold values from -1.8 to 1.8
- skip_gain: float32 [1024], P('tp'), may hold values from -4 to 4
- out_proj: bfloat16 [1024, 8192], P('tp', 'seq'), may hold values from -0.1875 to 0.1875
Outputs:
- mixed: bfloat16 [8192, 8192], P('seq', 'tp')
The draws below stay inside these ranges and needn't reach their ends.
All inputs are finite; a program needn't handle non-finite values.
Results may differ from the reference program's by a relative error of at most 0.007.
Values may be sent and summed in bfloat16 or wider, within the bound.
A program may use at most 64 MiB of HBM per device.

```python
import jax
import jax.numpy as jnp

D = 1024
D_MODEL = 8192
SHORT = 3
TOKENS = 8192


def draw_long_filter(key, part):
    position = jnp.arange(TOKENS, dtype=jnp.float32)[:, None]
    envelope = 0.3 * (1.0 + position) ** (-0.5)
    values = jnp.clip(jax.random.normal(key, (TOKENS, D), jnp.float32), -6.0, 6.0)
    return (values * envelope).astype(jnp.float32)


def levels(own_key, dims, cuts, least, top_value):
    factor_of = 1.0
    for dim, blocks in cuts:
        steps = jax.random.uniform(jax.random.fold_in(jax.random.fold_in(own_key, 6), dim), (blocks,), jnp.float32, least / len(cuts), top_value / len(cuts))
        factor_of = factor_of * jnp.repeat(jnp.exp(steps), dims[dim] // blocks).reshape((-1,) + (1,) * (len(dims) - 1 - dim))
    return factor_of


def bell_draw(key, extent, width, limit, split=(), kind=jnp.bfloat16):
    entries = jax.random.normal(key, extent, jnp.float32) * width
    if len(split) > 0:
        entries = levels(key, extent, split, -0.22, 0.18) * entries
    return jnp.clip(entries, min=-limit, max=limit).astype(kind)


def setup_inputs(seed: int = 0) -> dict:
    key_list = jax.random.split(jax.random.key(seed), 7)
    return {
        "features": bell_draw(key_list[0], (TOKENS, D_MODEL), 1.0, 6.0, ((0, 64), (1, 8))),
        "in_proj": bell_draw(key_list[1], (3, D_MODEL, D), D_MODEL ** -0.5, 0.0625, ((1, 64), (2, 8))),
        "short_taps": bell_draw(key_list[2], (3, SHORT, D), 0.5, 3.0, ((2, 8),), jnp.float32),
        "long_filter": draw_long_filter(jax.random.fold_in(key_list[6], 71), 0),
        "skip_gain": bell_draw(key_list[4], (D,), 1.0, 4.0, ((0, 8),), jnp.float32),
        "out_proj": bell_draw(key_list[5], (D, D_MODEL), D ** -0.5, 0.1875, ((0, 8), (1, 64))),
    }


def reference(features, in_proj, short_taps, long_filter, skip_gain, out_proj):
    projected = jnp.stack([jnp.dot(features, in_proj[stream], preferred_element_type=jnp.float32) for stream in range(3)]).astype(jnp.bfloat16)
    widened = projected.astype(jnp.float32)
    padded = jnp.pad(widened, ((0, 0), (SHORT - 1, 0), (0, 0)))
    filtered = jnp.zeros_like(widened)
    for offset in range(SHORT):
        begin = SHORT - 1 - offset
        filtered = filtered + short_taps[:, offset, None, :] * padded[:, begin:begin + TOKENS, :]
    query = filtered[0]
    inner = filtered[1] * filtered[2]
    pieces = []
    block = min(128, D)
    for start in range(0, D, block):
        spec_inner = jnp.fft.rfft(inner[:, start:start + block], n=2 * TOKENS, axis=0)
        spec_filter = jnp.fft.rfft(long_filter[:, start:start + block], n=2 * TOKENS, axis=0)
        pieces.append(jnp.fft.irfft(spec_inner * spec_filter, n=2 * TOKENS, axis=0)[:TOKENS].astype(jnp.float32))
    long_mix = jnp.concatenate(pieces, axis=1)
    gated = (query * (long_mix + skip_gain[None, :] * inner)).astype(jnp.bfloat16)
    return jnp.dot(gated, out_proj, preferred_element_type=jnp.float32).astype(jnp.bfloat16)
```

```python
import functools

import jax
import jax.numpy as jnp
from jax import lax
from jax.experimental import pallas as pl
from jax.experimental.pallas import tpu as pltpu
from jax.sharding import PartitionSpec as P

B = 128
HALO = 16
BF16, F32 = jnp.bfloat16, jnp.float32


def lanes(i):
    return pl.ds(pl.multiple_of(i * B, B), B)


def kernel(
    ny, nx, feat, win, taps, filt, skip, wout, out,
    F, Wb, Wc, Ps, Pr, Hr, pad, qi, Fs, Fr, Xs, Xr, Ys, Yr, Xp, A, T, Gs, Gt, Wo,
    loc, sF, rF, sW, rW, sZ, rZ, sC, rC, sP, rP, sH, rH, sV, rV, sG, rG, sO, rO,
):
    np_ = 2 * nx
    nq = 2 * nx
    nzl = np_ // 2
    ns = nq * ny
    cpd = B // ns
    s = lax.axis_index("seq")
    p = lax.axis_index("tp")
    q, y = s // ny, s % ny
    zl, c = p // 2, p % 2
    mate = p + 1 - 2 * c
    far = (q + nx) % nq

    def send(src, dst, ss, rs, sq, tp):
        pltpu.make_async_remote_copy(
            src_ref=src, dst_ref=dst, send_sem=ss, recv_sem=rs,
            device_id={"seq": sq, "tp": tp}, device_id_type=pl.DeviceIdType.MESH,
        ).start()

    def wait(ref, sem):
        pltpu.make_async_copy(ref, ref, sem).wait()

    def local(src, dst, sem):
        pltpu.make_async_copy(src, dst, sem).start()

    def loop(lo, hi, body):
        lax.fori_loop(lo, hi, lambda i, carry: (body(i), carry)[1], 0)

    barrier = pltpu.get_barrier_semaphore()

    def greet(sq, tp):
        pl.semaphore_signal(
            barrier, inc=1, device_id={"seq": sq, "tp": tp}, device_id_type=pl.DeviceIdType.MESH
        )

    loop(1, ns, lambda k: greet((s + k) % ns, p))
    loop(1, np_, lambda k: greet(s, (p + k) % np_))

    @pl.when(q != p)
    def _():
        greet(p * ny + y, q)

    turned = filt[...].T
    for k in range(cpd):
        Fs[:, k, :] = turned[k * ns:(k + 1) * ns]
    Fr[pl.ds(s, 1)] = Fs[pl.ds(s, 1)]
    local(feat.at[:, lanes(y)], F.at[y, :, lanes(p)], loc.at[0])
    local(win, Wb.at[q], loc.at[1])

    @pl.when(q == p)
    def _():
        local(wout, Wo.at[lanes(q), lanes(y)], loc.at[2])

    pl.semaphore_wait(barrier, ns - 1 + np_ - 1 + jnp.where(q == p, 0, 1))

    def block_of(i):
        half = (i + 1) // 2
        return (y + half * (2 * (i % 2) - 1) + ny) % ny

    def spread(i):
        to = block_of(i)
        send(feat.at[:, lanes(to)], F.at[y, :, lanes(p)], sF, rF.at[y], q * ny + to, p)

    loop(1, ny, spread)
    send(win, Wb.at[q], sW, rW.at[0], far * ny + y, p)

    @pl.when(q != p)
    def _():
        send(wout, Wo.at[lanes(p), lanes(y)], sO.at[0], rO.at[0], p * ny + y, q)

    loop(1, ns, lambda k: send(Fs.at[(s + k) % ns], Fr.at[s], sV.at[0], rV.at[0], (s + k) % ns, p))

    def forward(tb):
        mine = F.at[tb, :, lanes(p)]
        for k in range(1, nzl):
            send(mine, mine, sZ, rZ.at[tb], s, ((zl + k) % nzl) * 2 + c)
        send(mine, mine, sC, rC.at[tb], s, mate)

    wait(F.at[0, :, pl.ds(0, B)], loc.at[0])
    wait(win, loc.at[1])
    forward(y)

    wait(Wb.at[0], rW.at[0])

    def weights(k):
        x = q % nx
        to = (q - x) + (x + k) % nx
        send(Wb.at[q], Wb.at[q], sW, rW.at[1], to * ny + y, p)
        send(Wb.at[far], Wb.at[far], sW, rW.at[1], to * ny + y, p)

    loop(1, nx, weights)

    def pass_on(i):
        tb = block_of(i)
        wait(F.at[0, :, pl.ds(0, B)], rF.at[tb])
        forward(tb)

    loop(1, ny, pass_on)

    @pl.when(q == p)
    def _():
        wait(wout, loc.at[2])

    @pl.when(q != p)
    def _():
        wait(wout, rO.at[0])

    own_o = Wo.at[lanes(q), lanes(y)]
    far_o = Wo.at[lanes(far), lanes(y)]
    send(own_o, own_o, sO.at[1], rO.at[1], far * ny + y, p)

    wait(Fr.at[pl.ds(0, ns - 1)], rV.at[0])
    row = lax.broadcasted_iota(jnp.int32, (B, B), 0)
    col = lax.broadcasted_iota(jnp.int32, (B, B), 1)
    causal = col >= row
    per = ns // ny

    def toeplitz(i):
        for ch in range(cpd):
            def circulant(d):
                line = jnp.broadcast_to(Fr[pl.ds(d, 1), ch, :], (B, B))
                return pltpu.roll(line, 0, 1, stride=1, stride_axis=0)

            before = circulant(jnp.maximum(i * per - 1, 0))
            before = jnp.where(i == 0, jnp.zeros_like(before), before)

            def step(j, before):
                d = i * per + j
                now = circulant(d)
                T[ch, lanes(d), :] = jnp.where(causal, now, before).astype(BF16)
                return now

            lax.fori_loop(0, per, step, before)

    def relay(tb):
        wait(F.at[0, :, pl.ds(0, (nzl - 1) * B)], rZ.at[tb])
        for k in range(1, nzl):
            other = F.at[tb, :, lanes(((zl + k) % nzl) * 2 + c)]
            send(other, other, sC, rC.at[tb], s, mate)

    def halo_to(tb):
        return q * ny + tb + 1

    @pl.when(s == 0)
    def _():
        Hr[...] = jnp.zeros_like(Hr)

    def project(tb, own):
        wait(F.at[0, :, pl.ds(0, nzl * B)], rC.at[tb])
        Ps[tb] = jnp.dot(F[tb], Wc[...], preferred_element_type=F32).astype(BF16)
        if own:
            Pr[y] = Ps[tb]
        else:
            send(Ps.at[tb], Pr.at[y], sP, rP, q * ny + tb, p)

        @pl.when(tb + 1 == y)
        def _():
            Hr[y] = Ps[tb, B - HALO:, :]

        @pl.when((tb + 1 != y) & (halo_to(tb) < ns))
        def _():
            send(Ps.at[tb, pl.ds(B - HALO, HALO), :], Hr.at[y], sH.at[tb], rH, halo_to(tb), p)

    relay(y)
    wait(Wb.at[pl.ds(0, np_ - 2)], rW.at[1])
    for k in range(np_):
        for stream in range(3):
            Wc[k * B:(k + 1) * B, stream * B:(stream + 1) * B] = Wb[k, stream]
    toeplitz(0)

    def main(i):
        relay(block_of(i))
        @pl.when(i == 1)
        def _():
            project(y, True)
        @pl.when(i > 1)
        def _():
            project(block_of(i - 1), False)
        toeplitz(i)

    loop(1, ny, main)
    project(block_of(ny - 1), False)

    wait(wout, rO.at[1])

    def along_y(k):
        to = q * ny + (y + k) % ny
        send(own_o, own_o, sO.at[2], rO.at[2], to, p)
        send(far_o, far_o, sO.at[2], rO.at[2], to, p)

    loop(1, ny, along_y)

    wait(Pr.at[pl.ds(0, ny - 1)], rP)

    @pl.when(y > 0)
    def _():
        wait(Hr.at[pl.ds(0, ny - 1)], rH)

    @pl.when((y == 0) & (q > 0))
    def _():
        wait(Hr.at[pl.ds(0, ny)], rH)

    full = Pr[0].astype(F32)
    head = Hr[0].astype(F32)
    for k in range(1, ny):
        full = full + Pr[k].astype(F32)
        head = head + Hr[k].astype(F32)
    pad[HALO:] = full.astype(BF16).astype(F32)
    pad[:HALO] = head.astype(BF16).astype(F32)
    streams = []
    for stream in range(3):
        own = slice(stream * B, (stream + 1) * B)
        total = jnp.zeros((B, B), F32)
        for j in range(3):
            total = total + taps[stream, j:j + 1, :] * pad[HALO - j:HALO - j + B, own]
        streams.append(total)
    inner = streams[1] * streams[2]
    qi[0] = streams[0]
    qi[1] = inner

    turned = inner.T
    for k in range(cpd):
        Xs[:, k, :] = turned[k * ns:(k + 1) * ns]
    Xr[pl.ds(s, 1)] = Xs[pl.ds(s, 1)]
    loop(1, ns, lambda k: send(Xs.at[(s + k) % ns], Xr.at[s], sV.at[1], rV.at[1], (s + k) % ns, p))
    Xp[:ns] = jnp.zeros((ns, B), F32)

    wait(Wo.at[pl.ds(0, 2 * B), pl.ds(0, (ny - 1) * B)], rO.at[2])

    def along_x(k):
        x = q % nx
        to = ((q - x) + (x + k) % nx) * ny + y
        send(Wo.at[lanes(q)], Wo.at[lanes(q)], sO.at[3], rO.at[3], to, p)
        send(Wo.at[lanes(far)], Wo.at[lanes(far)], sO.at[3], rO.at[3], to, p)

    loop(1, nx, along_x)

    wait(Xr.at[pl.ds(0, ns - 1)], rV.at[1])
    for ch in range(cpd):
        Xp[ns:] = Xr[:, ch, :]
        for d in range(ns):
            A[:, d * B:(d + 1) * B] = Xp[ns - d:2 * ns - d].astype(BF16)
        Ys[:, ch, :] = jnp.dot(A[...], T[ch], preferred_element_type=F32)
    Yr[pl.ds(s, 1)] = Ys[pl.ds(s, 1)]
    loop(1, ns, lambda k: send(Ys.at[(s + k) % ns], Yr.at[s], sV.at[2], rV.at[2], (s + k) % ns, p))
    wait(Yr.at[pl.ds(0, ns - 1)], rV.at[2])
    mix = jnp.concatenate([Yr[:, ch, :] for ch in range(cpd)], axis=0).T
    Gs[...] = (qi[0] * (mix + skip[...] * qi[1])).astype(BF16)

    loop(1, np_, lambda k: send(Gs, Gt.at[:, lanes(p)], sG, rG, s, (p + k) % np_))
    local(Gs, Gt.at[:, lanes(p)], loc.at[3])
    wait(Wo.at[pl.ds(0, (np_ - 2) * B)], rO.at[3])
    wait(Gs, loc.at[3])
    wait(Gt.at[:, pl.ds(0, (np_ - 1) * B)], rG)
    out[...] = jnp.dot(Gt[...], Wo[...], preferred_element_type=F32).astype(BF16)

    wait(F.at[pl.ds(0, ny - 1), :, pl.ds(0, B)], sF)
    wait(Wb.at[pl.ds(0, np_ - 1)], sW)
    wait(F.at[:, :, pl.ds(0, (nzl - 1) * B)], sZ)
    wait(F.at[:, :, pl.ds(0, nzl * B)], sC)
    wait(Pr.at[pl.ds(0, ny - 1)], sP)

    def halo_sent(tb):
        @pl.when((tb + 1 != y) & (halo_to(tb) < ns))
        def _():
            wait(Hr.at[0], sH.at[tb])

    loop(0, ny, halo_sent)
    for k in range(3):
        wait(Xs.at[pl.ds(0, ns - 1)], sV.at[k])
    wait(Gt.at[:, pl.ds(0, (np_ - 1) * B)], sG)

    @pl.when(q != p)
    def _():
        wait(wout, sO.at[0])

    wait(wout, sO.at[1])
    wait(Wo.at[pl.ds(0, 2 * B), pl.ds(0, (ny - 1) * B)], sO.at[2])
    wait(Wo.at[pl.ds(0, (np_ - 2) * B)], sO.at[3])


def per_device(features, in_proj, short_taps, long_filter, skip_gain, out_proj):
    ns, np_ = lax.axis_size("seq"), lax.axis_size("tp")
    nx = np_ // 2
    ny = ns // np_
    cpd = B // ns
    dma = pltpu.SemaphoreType.DMA
    rows = pltpu.VMEM((ns, cpd, B), F32)
    return pl.pallas_call(
        functools.partial(kernel, ny, nx),
        out_shape=jax.ShapeDtypeStruct((B, ny * B), BF16),
        in_specs=[pl.BlockSpec(memory_space=pltpu.VMEM)] * 6,
        out_specs=pl.BlockSpec(memory_space=pltpu.VMEM),
        scratch_shapes=[
            pltpu.VMEM((ny, B, np_ * B), BF16),
            pltpu.VMEM((np_, 3, B, B), BF16),
            pltpu.VMEM((np_ * B, 3 * B), BF16),
            pltpu.VMEM((ny, B, 3 * B), BF16),
            pltpu.VMEM((ny, B, 3 * B), BF16),
            pltpu.VMEM((ny, HALO, 3 * B), BF16),
            pltpu.VMEM((HALO + B, 3 * B), F32),
            pltpu.VMEM((2, B, B), F32),
            rows, rows, rows, rows, rows, rows,
            pltpu.VMEM((2 * ns, B), F32),
            pltpu.VMEM((ns, ns * B), BF16),
            pltpu.VMEM((cpd, ns * B, B), BF16),
            pltpu.VMEM((B, B), BF16),
            pltpu.VMEM((B, np_ * B), BF16),
            pltpu.VMEM((np_ * B, ny * B), BF16),
            dma((4,)),
            dma, dma((ny,)),
            dma, dma((2,)),
            dma, dma((ny,)),
            dma, dma((ny,)),
            dma, dma,
            dma((ny,)), dma,
            dma((3,)), dma((3,)),
            dma, dma,
            dma((4,)), dma((4,)),
        ],
        compiler_params=pltpu.CompilerParams(
            collective_id=0, has_side_effects=True, vmem_limit_bytes=48 * 1024 * 1024
        ),
        name="operator",
    )(features, in_proj, short_taps, long_filter, skip_gain.reshape(1, B), out_proj)


def solution(mesh):
    return jax.shard_map(
        per_device,
        mesh=mesh,
        in_specs=(
            P("seq", "tp"),
            P(None, "seq", "tp"),
            P(None, None, "tp"),
            P("seq", "tp"),
            P("tp"),
            P("tp", "seq"),
        ),
        out_specs=P("seq", "tp"),
        check_vma=False,
    )
```

```python
import functools

import jax
import jax.numpy as jnp
from jax import lax
from jax.experimental import pallas as pl
from jax.experimental.pallas import tpu as pltpu
from jax.sharding import PartitionSpec as P

B = 128
HALO = 16
BF16, F32 = jnp.bfloat16, jnp.float32


def lanes(i):
    return pl.ds(pl.multiple_of(i * B, B), B)


def kernel(
    ny, nx, feat_h, win_h, taps_h, filt_h, skip_h, wout_h, out,
    feat, win, taps, filt, skip, wout,
    F, Wb, Wc, Ps, Pr, Hr, pad, qi, Fs, Fr, Xs, Xr, Ys, Yr, Xp, A, T, Gs, Gt, Wo,
    arg, loc, sF, rF, sW, rW, sZ, rZ, sE, rE, sC, rC, sP, rP, sH, rH, sV, rV, sG, rG, sO, rO,
):
    np_ = 2 * nx
    nq = 2 * nx
    nzl = np_ // 2
    ns = nq * ny
    cpd = B // ns
    s = lax.axis_index("seq")
    p = lax.axis_index("tp")
    q, y = s // ny, s % ny
    zl, c = p // 2, p % 2
    mate = p + 1 - 2 * c
    far = (q + nx) % nq
    chain = nzl == 4
    end = (zl == 0) | (zl == nzl - 1)

    def send(src, dst, ss, rs, sq, tp):
        pltpu.make_async_remote_copy(
            src_ref=src, dst_ref=dst, send_sem=ss, recv_sem=rs,
            device_id={"seq": sq, "tp": tp}, device_id_type=pl.DeviceIdType.MESH,
        ).start()

    def wait(ref, sem):
        pltpu.make_async_copy(ref, ref, sem).wait()

    def local(src, dst, sem):
        pltpu.make_async_copy(src, dst, sem).start()

    def loop(lo, hi, body):
        lax.fori_loop(lo, hi, lambda i, carry: (body(i), carry)[1], 0)

    def away(k):
        return (s + (k + ns // 3) % (ns - 1) + 1) % ns

    local(filt_h, filt, arg.at[0])
    local(feat_h, feat, arg.at[1])
    local(win_h, win, arg.at[2])
    local(wout_h, wout, arg.at[3])
    local(taps_h, taps, arg.at[4])
    local(skip_h, skip, arg.at[5])

    barrier = pltpu.get_barrier_semaphore()

    def greet(sq, tp):
        pl.semaphore_signal(
            barrier, inc=1, device_id={"seq": sq, "tp": tp}, device_id_type=pl.DeviceIdType.MESH
        )

    loop(0, ns - 1, lambda k: greet(away(k), p))
    greet(p * ny + y, far)

    @pl.when(q != p)
    def _():
        greet(p * ny + y, q)

    loop(1, np_, lambda k: greet(s, (p + k) % np_))

    wait(feat, arg.at[1])
    wait(win, arg.at[2])
    wait(wout, arg.at[3])
    local(feat.at[:, lanes(y)], F.at[y, :, lanes(p)], loc.at[0])
    local(win, Wb.at[q], loc.at[1])

    @pl.when(q == p)
    def _():
        local(wout, Wo.at[lanes(q), lanes(y)], loc.at[2])

    wait(filt, arg.at[0])
    turned = filt[...].T
    for k in range(cpd):
        Fs[:, k, :] = turned[k * ns:(k + 1) * ns]
    Fr[pl.ds(s, 1)] = Fs[pl.ds(s, 1)]
    wait(taps, arg.at[4])
    wait(skip, arg.at[5])
    wait(F.at[0, :, pl.ds(0, B)], loc.at[0])
    wait(win, loc.at[1])

    @pl.when(q == p)
    def _():
        wait(wout, loc.at[2])

    pl.semaphore_wait(barrier, ns + np_ - 1 + jnp.where(q == p, 0, 1))

    def block_of(i):
        half = jnp.where(i < 3, (i + 1) // 2, ny // 2 - (i - 2) // 2)
        sign = jnp.where(i < 3, 2 * (i % 2) - 1, 1 - 2 * (i % 2))
        return (y + half * sign + ny) % ny

    def spread(i):
        to = block_of(i)
        send(feat.at[:, lanes(to)], F.at[y, :, lanes(p)], sF, rF.at[y], q * ny + to, p)

    def forward(tb):
        mine = F.at[tb, :, lanes(p)]
        for k in range(1, nzl):
            to = (zl + k) % nzl
            if chain:
                @pl.when((to - zl != 3) & (zl - to != 3))
                def _():
                    send(mine, mine, sZ, rZ.at[tb], s, to * 2 + c)
            else:
                send(mine, mine, sZ, rZ.at[tb], s, to * 2 + c)
        send(mine, mine, sC, rC.at[tb], s, mate)

    def pass_on(i):
        tb = block_of(i)
        wait(F.at[0, :, pl.ds(0, B)], rF.at[tb])
        forward(tb)

    def blocks(n):
        return F.at[0, :, pl.ds(0, n * B)]

    def relay(tb):
        def block(z):
            return F.at[tb, :, lanes(z * 2 + c)]

        if not chain:
            wait(blocks(nzl - 1), rZ.at[tb])
            for k in range(1, nzl):
                other = block((zl + k) % nzl)
                send(other, other, sC, rC.at[tb], s, mate)
            return

        @pl.when(end)
        def _():
            wait(blocks(2), rZ.at[tb])
            for k in range(1, 3):
                other = block(jnp.where(zl == 0, k, 3 - k))
                send(other, other, sC, rC.at[tb], s, mate)

        @pl.when(jnp.logical_not(end))
        def _():
            wait(blocks(3), rZ.at[tb])
            other = block(3 * (2 - zl))
            send(other, other, sE, rE.at[tb], s, 3 * (zl - 1) * 2 + c)
            for k in range(1, 4):
                other = block((zl + k) % 4)
                send(other, other, sC, rC.at[tb], s, mate)

    def last_leg(tb):
        if not chain:
            return

        @pl.when(end)
        def _():
            wait(blocks(1), rE.at[tb])
            other = F.at[tb, :, lanes((3 - zl) * 2 + c)]
            send(other, other, sC, rC.at[tb], s, mate)

    loop(1, ny, spread)
    send(win, Wb.at[q], sW, rW.at[0], far * ny + y, p)
    forward(y)

    @pl.when(q != p)
    def _():
        send(wout, Wo.at[lanes(p), lanes(y)], sO.at[0], rO.at[0], p * ny + y, q)

    send(wout, Wo.at[lanes(p), lanes(y)], sO.at[1], rO.at[1], ((p + nx) % nq) * ny + y, q)
    loop(1, min(3, ny), pass_on)

    wait(Wb.at[0], rW.at[0])

    def weights(k):
        x = q % nx
        to = (q - x) + (x + k) % nx
        send(Wb.at[q], Wb.at[q], sW, rW.at[1], to * ny + y, p)
        send(Wb.at[far], Wb.at[far], sW, rW.at[1], to * ny + y, p)

    loop(1, nx, weights)
    loop(min(3, ny), ny, pass_on)

    @pl.when(q != p)
    def _():
        wait(wout, rO.at[0])

    wait(wout, rO.at[1])
    own_o = Wo.at[lanes(q), lanes(y)]
    far_o = Wo.at[lanes(far), lanes(y)]

    def along_y(k):
        to = q * ny + (y + k) % ny
        send(own_o, own_o, sO.at[2], rO.at[2], to, p)
        send(far_o, far_o, sO.at[2], rO.at[2], to, p)

    loop(1, ny, along_y)
    loop(0, ns - 1, lambda k: send(Fs.at[away(k)], Fr.at[s], sV.at[0], rV.at[0], away(k), p))

    row = lax.broadcasted_iota(jnp.int32, (B, B), 0)
    col = lax.broadcasted_iota(jnp.int32, (B, B), 1)
    causal = col >= row
    per = ns // 8

    def toeplitz(i):
        for ch in range(cpd):
            def circulant(d):
                line = jnp.broadcast_to(Fr[pl.ds(d, 1), ch, :], (B, B))
                return pltpu.roll(line, 0, 1, stride=1, stride_axis=0)

            before = circulant(jnp.maximum(i * per - 1, 0))
            before = jnp.where(i == 0, jnp.zeros_like(before), before)

            def step(j, before):
                d = i * per + j
                now = circulant(d)
                T[ch, lanes(d), :] = jnp.where(causal, now, before).astype(BF16)
                return now

            lax.fori_loop(0, per, step, before)

    def halo_to(tb):
        return q * ny + tb + 1

    @pl.when(s == 0)
    def _():
        Hr[...] = jnp.zeros_like(Hr)

    def project(tb, own):
        wait(blocks(nzl), rC.at[tb])
        Ps[tb] = jnp.dot(F[tb], Wc[...], preferred_element_type=F32).astype(BF16)
        if own:
            Pr[y] = Ps[tb]
        else:
            send(Ps.at[tb], Pr.at[y], sP, rP, q * ny + tb, p)

        @pl.when(tb + 1 == y)
        def _():
            Hr[y] = Ps[tb, B - HALO:, :]

        @pl.when((tb + 1 != y) & (halo_to(tb) < ns))
        def _():
            send(Ps.at[tb, pl.ds(B - HALO, HALO), :], Hr.at[y], sH.at[tb], rH, halo_to(tb), p)

    relay(y)
    wait(Wb.at[pl.ds(0, np_ - 2)], rW.at[1])
    for k in range(np_):
        for stream in range(3):
            Wc[k * B:(k + 1) * B, stream * B:(stream + 1) * B] = Wb[k, stream]

    def along_x(k):
        x = q % nx
        to = ((q - x) + (x + k) % nx) * ny + y
        send(Wo.at[lanes(q)], Wo.at[lanes(q)], sO.at[3], rO.at[3], to, p)
        send(Wo.at[lanes(far)], Wo.at[lanes(far)], sO.at[3], rO.at[3], to, p)

    def main(i):
        relay(block_of(i))
        last_leg(block_of(i - 1))

        @pl.when(i == 2)
        def _():
            project(y, True)

        @pl.when(i > 2)
        def _():
            project(block_of(i - 2), False)

        @pl.when(i == min(3, ny - 1))
        def _():
            wait(Wo.at[pl.ds(0, 2 * B), pl.ds(0, (ny - 1) * B)], rO.at[2])
            loop(1, nx, along_x)
            wait(Fr.at[pl.ds(0, ns - 1)], rV.at[0])

        @pl.when(i >= 4)
        def _():
            toeplitz(i - 4)

    loop(1, ny, main)
    last_leg(block_of(ny - 1))
    if ny > 2:
        project(block_of(ny - 2), False)
    else:
        project(y, True)
    project(block_of(ny - 1), False)
    loop(max(ny - 4, 0), 6, toeplitz)

    wait(Pr.at[pl.ds(0, ny - 1)], rP)

    @pl.when(y > 0)
    def _():
        wait(Hr.at[pl.ds(0, ny - 1)], rH)

    @pl.when((y == 0) & (q > 0))
    def _():
        wait(Hr.at[pl.ds(0, ny)], rH)

    full = Pr[0].astype(F32)
    head = Hr[0].astype(F32)
    for k in range(1, ny):
        full = full + Pr[k].astype(F32)
        head = head + Hr[k].astype(F32)
    pad[HALO:] = full
    pad[:HALO] = head
    streams = []
    for stream in range(3):
        own = slice(stream * B, (stream + 1) * B)
        total = jnp.zeros((B, B), F32)
        for j in range(3):
            total = total + taps[stream, j:j + 1, :] * pad[HALO - j:HALO - j + B, own]
        streams.append(total)
    inner = streams[1] * streams[2]
    qi[0] = streams[0]
    qi[1] = inner

    turned = inner.T
    for k in range(cpd):
        Xs[:, k, :] = turned[k * ns:(k + 1) * ns]
    Xr[pl.ds(s, 1)] = Xs[pl.ds(s, 1)]
    loop(0, ns - 1, lambda k: send(Xs.at[away(k)], Xr.at[s], sV.at[1], rV.at[1], away(k), p))
    Xp[:ns] = jnp.zeros((ns, B), F32)
    loop(6, 8, toeplitz)

    wait(Xr.at[pl.ds(0, ns - 1)], rV.at[1])
    for ch in range(cpd):
        Xp[ns:] = Xr[:, ch, :]
        for d in range(ns):
            A[:, d * B:(d + 1) * B] = Xp[ns - d:2 * ns - d].astype(BF16)
        Ys[:, ch, :] = jnp.dot(A[...], T[ch], preferred_element_type=F32)
    Yr[pl.ds(s, 1)] = Ys[pl.ds(s, 1)]
    loop(0, ns - 1, lambda k: send(Ys.at[away(k)], Yr.at[s], sV.at[2], rV.at[2], away(k), p))
    wait(Yr.at[pl.ds(0, ns - 1)], rV.at[2])
    mix = jnp.concatenate([Yr[:, ch, :] for ch in range(cpd)], axis=0).T
    Gs[...] = (qi[0] * (mix + skip[...] * qi[1])).astype(BF16)

    gated = Gt.at[:, lanes(p)]
    for k in range(1, nzl):
        send(Gs, gated, sG, rG.at[0], s, ((zl + k) % nzl) * 2 + c)
    send(Gs, gated, sG, rG.at[1], s, mate)
    local(Gs, gated, loc.at[0])
    wait(Wo.at[pl.ds(0, (np_ - 2) * B)], rO.at[3])
    wait(Gs, loc.at[0])
    wait(Gt.at[:, pl.ds(0, (nzl - 1) * B)], rG.at[0])
    for k in range(1, nzl):
        other = Gt.at[:, lanes(((zl + k) % nzl) * 2 + c)]
        send(other, other, sG, rG.at[1], s, mate)
    wait(Gt.at[:, pl.ds(0, nzl * B)], rG.at[1])
    out[...] = jnp.dot(Gt[...], Wo[...], preferred_element_type=F32).astype(BF16)

    wait(F.at[pl.ds(0, ny - 1), :, pl.ds(0, B)], sF)
    wait(Wb.at[pl.ds(0, np_ - 1)], sW)
    if chain:
        @pl.when(end)
        def _():
            wait(F.at[:, :, pl.ds(0, 2 * B)], sZ)

        @pl.when(jnp.logical_not(end))
        def _():
            wait(F.at[:, :, pl.ds(0, 3 * B)], sZ)
            wait(F.at[:, :, pl.ds(0, B)], sE)
    else:
        wait(F.at[:, :, pl.ds(0, (nzl - 1) * B)], sZ)
    wait(F.at[:, :, pl.ds(0, nzl * B)], sC)
    wait(Pr.at[pl.ds(0, ny - 1)], sP)

    def halo_sent(tb):
        @pl.when((tb + 1 != y) & (halo_to(tb) < ns))
        def _():
            wait(Hr.at[0], sH.at[tb])

    loop(0, ny, halo_sent)
    for k in range(3):
        wait(Xs.at[pl.ds(0, ns - 1)], sV.at[k])
    wait(Gt.at[:, pl.ds(0, (2 * nzl - 1) * B)], sG)

    @pl.when(q != p)
    def _():
        wait(wout, sO.at[0])

    wait(wout, sO.at[1])
    wait(Wo.at[pl.ds(0, 2 * B), pl.ds(0, (ny - 1) * B)], sO.at[2])
    wait(Wo.at[pl.ds(0, (np_ - 2) * B)], sO.at[3])


def per_device(features, in_proj, short_taps, long_filter, skip_gain, out_proj):
    ns, np_ = lax.axis_size("seq"), lax.axis_size("tp")
    nx = np_ // 2
    ny = ns // np_
    cpd = B // ns
    dma = pltpu.SemaphoreType.DMA
    rows = pltpu.VMEM((ns, cpd, B), F32)
    return pl.pallas_call(
        functools.partial(kernel, ny, nx),
        out_shape=jax.ShapeDtypeStruct((B, ny * B), BF16),
        in_specs=[pl.BlockSpec(memory_space=pl.ANY)] * 6,
        out_specs=pl.BlockSpec(memory_space=pltpu.VMEM),
        scratch_shapes=[
            pltpu.VMEM((B, ny * B), BF16),
            pltpu.VMEM((3, B, B), BF16),
            pltpu.VMEM((3, 3, B), F32),
            pltpu.VMEM((B, B), F32),
            pltpu.VMEM((1, B), F32),
            pltpu.VMEM((B, B), BF16),
            pltpu.VMEM((ny, B, np_ * B), BF16),
            pltpu.VMEM((np_, 3, B, B), BF16),
            pltpu.VMEM((np_ * B, 3 * B), BF16),
            pltpu.VMEM((ny, B, 3 * B), BF16),
            pltpu.VMEM((ny, B, 3 * B), BF16),
            pltpu.VMEM((ny, HALO, 3 * B), BF16),
            pltpu.VMEM((HALO + B, 3 * B), F32),
            pltpu.VMEM((2, B, B), F32),
            rows, rows, rows, rows, rows, rows,
            pltpu.VMEM((2 * ns, B), F32),
            pltpu.VMEM((ns, ns * B), BF16),
            pltpu.VMEM((cpd, ns * B, B), BF16),
            pltpu.VMEM((B, B), BF16),
            pltpu.VMEM((B, np_ * B), BF16),
            pltpu.VMEM((np_ * B, ny * B), BF16),
            dma((6,)), dma((3,)),
            dma, dma((ny,)),
            dma, dma((2,)),
            dma, dma((ny,)),
            dma, dma((ny,)),
            dma, dma((ny,)),
            dma, dma,
            dma((ny,)), dma,
            dma((3,)), dma((3,)),
            dma, dma((2,)),
            dma((4,)), dma((4,)),
        ],
        compiler_params=pltpu.CompilerParams(
            collective_id=0, has_side_effects=True
        ),
        name="operator",
    )(features, in_proj, short_taps, long_filter, skip_gain.reshape(1, B), out_proj)


def solution(mesh):
    return jax.shard_map(
        per_device,
        mesh=mesh,
        in_specs=(
            P("seq", "tp"),
            P(None, "seq", "tp"),
            P(None, None, "tp"),
            P("seq", "tp"),
            P("tp"),
            P("tp", "seq"),
        ),
        out_specs=P("seq", "tp"),
        check_vma=False,
    )
```

```python
import functools

import jax
import jax.numpy as jnp
from jax import lax
from jax.experimental import pallas as pl
from jax.experimental.pallas import tpu as pltpu
from jax.sharding import PartitionSpec as P

B = 128
HALO = 16
BF16, F32 = jnp.bfloat16, jnp.float32


def lanes(i):
    return pl.ds(pl.multiple_of(i * B, B), B)


def kernel(
    ny, nx, feat_h, win_h, taps_h, filt_h, skip_h, wout_h, out,
    feat, win, taps, filt, skip, wout,
    F, Wb, Wc, Ps, Pr, Hr, pad, qi, Fs, Fr, Xs, Xr, Ys, Yr, Xp, A, T, Gs, Gt, Wo,
    arg, loc, sF, rF, sW, rW, sZ, rZ, sE, rE, sC, rC, sP, rP, sH, rH, sV, rV, sG, rG, sO, rO, rU, rD,
):
    np_ = 2 * nx
    nq = 2 * nx
    nzl = np_ // 2
    ns = nq * ny
    cpd = B // ns
    s = lax.axis_index("seq")
    p = lax.axis_index("tp")
    q, y = s // ny, s % ny
    zl, c = p // 2, p % 2
    mate = p + 1 - 2 * c
    far = (q + nx) % nq
    chain = nzl == 4
    end = (zl == 0) | (zl == nzl - 1)

    def send(src, dst, ss, rs, sq, tp):
        pltpu.make_async_remote_copy(
            src_ref=src, dst_ref=dst, send_sem=ss, recv_sem=rs,
            device_id={"seq": sq, "tp": tp}, device_id_type=pl.DeviceIdType.MESH,
        ).start()

    def wait(ref, sem):
        pltpu.make_async_copy(ref, ref, sem).wait()

    def local(src, dst, sem):
        pltpu.make_async_copy(src, dst, sem).start()

    def loop(lo, hi, body):
        lax.fori_loop(lo, hi, lambda i, carry: (body(i), carry)[1], 0)

    def away(k):
        return (s + (k + ns // 3) % (ns - 1) + 1) % ns

    local(filt_h, filt, arg.at[0])
    local(feat_h, feat, arg.at[1])
    local(win_h, win, arg.at[2])
    local(wout_h, wout, arg.at[3])
    local(taps_h, taps, arg.at[4])
    local(skip_h, skip, arg.at[5])

    barrier = pltpu.get_barrier_semaphore()

    def greet(sq, tp):
        pl.semaphore_signal(
            barrier, inc=1, device_id={"seq": sq, "tp": tp}, device_id_type=pl.DeviceIdType.MESH
        )

    loop(0, ns - 1, lambda k: greet(away(k), p))
    greet(p * ny + y, far)

    @pl.when(q != p)
    def _():
        greet(p * ny + y, q)

    loop(1, np_, lambda k: greet(s, (p + k) % np_))

    wait(feat, arg.at[1])
    wait(win, arg.at[2])
    wait(wout, arg.at[3])
    local(feat.at[:, lanes(y)], F.at[y, :, lanes(p)], loc.at[0])
    local(win, Wb.at[q], loc.at[1])

    @pl.when(q == p)
    def _():
        local(wout, Wo.at[lanes(q), lanes(y)], loc.at[2])

    wait(filt, arg.at[0])
    turned = filt[...].T
    for k in range(cpd):
        Fs[:, k, :] = turned[k * ns:(k + 1) * ns]
    Fr[pl.ds(s, 1)] = Fs[pl.ds(s, 1)]
    wait(taps, arg.at[4])
    wait(skip, arg.at[5])
    wait(F.at[0, :, pl.ds(0, B)], loc.at[0])
    wait(win, loc.at[1])

    @pl.when(q == p)
    def _():
        wait(wout, loc.at[2])

    pl.semaphore_wait(barrier, ns + np_ - 1 + jnp.where(q == p, 0, 1))

    def block_of(i):
        half = jnp.where(i < 3, (i + 1) // 2, ny // 2 - (i - 2) // 2)
        sign = jnp.where(i < 3, 2 * (i % 2) - 1, 1 - 2 * (i % 2))
        return (y + half * sign + ny) % ny

    def spread(i):
        to = block_of(i)
        send(feat.at[:, lanes(to)], F.at[y, :, lanes(p)], sF, rF.at[y], q * ny + to, p)

    def forward(tb):
        mine = F.at[tb, :, lanes(p)]
        for k in range(1, nzl):
            to = (zl + k) % nzl
            if chain:
                @pl.when((to - zl != 3) & (zl - to != 3))
                def _():
                    send(mine, mine, sZ, rZ.at[tb], s, to * 2 + c)
            else:
                send(mine, mine, sZ, rZ.at[tb], s, to * 2 + c)
        send(mine, mine, sC, rC.at[tb], s, mate)

    def pass_on(i):
        tb = block_of(i)
        wait(F.at[0, :, pl.ds(0, B)], rF.at[tb])
        forward(tb)

    def blocks(n):
        return F.at[0, :, pl.ds(0, n * B)]

    def relay(tb):
        def block(z):
            return F.at[tb, :, lanes(z * 2 + c)]

        if not chain:
            wait(blocks(nzl - 1), rZ.at[tb])
            for k in range(1, nzl):
                other = block((zl + k) % nzl)
                send(other, other, sC, rC.at[tb], s, mate)
            return

        @pl.when(end)
        def _():
            wait(blocks(2), rZ.at[tb])
            for k in range(1, 3):
                other = block(jnp.where(zl == 0, k, 3 - k))
                send(other, other, sC, rC.at[tb], s, mate)

        @pl.when(jnp.logical_not(end))
        def _():
            wait(blocks(3), rZ.at[tb])
            other = block(3 * (2 - zl))
            send(other, other, sE, rE.at[tb], s, 3 * (zl - 1) * 2 + c)
            for k in range(1, 4):
                other = block((zl + k) % 4)
                send(other, other, sC, rC.at[tb], s, mate)

    def last_leg(tb):
        if not chain:
            return

        @pl.when(end)
        def _():
            wait(blocks(1), rE.at[tb])
            other = F.at[tb, :, lanes((3 - zl) * 2 + c)]
            send(other, other, sC, rC.at[tb], s, mate)

    loop(1, ny, spread)
    send(win, Wb.at[q], sW, rW.at[0], far * ny + y, p)
    forward(y)

    def weights(which, sem):
        def step(k):
            x = q % nx
            to = (q - x) + (x + k) % nx
            send(Wb.at[which], Wb.at[which], sW, sem, to * ny + y, p)

        loop(1, nx, step)

    weights(q, rW.at[1])

    @pl.when(q != p)
    def _():
        send(wout, Wo.at[lanes(p), lanes(y)], sO.at[0], rO.at[0], p * ny + y, q)

    send(wout, Wo.at[lanes(p), lanes(y)], sO.at[1], rO.at[1], ((p + nx) % nq) * ny + y, q)
    loop(1, ny, pass_on)
    wait(Wb.at[0], rW.at[0])
    weights(far, rW.at[2])

    @pl.when(q != p)
    def _():
        wait(wout, rO.at[0])

    wait(wout, rO.at[1])
    reach = ny // 2
    x_pos = q % nx
    right = ((q - x_pos) + (x_pos + 1) % nx) * ny + y
    left = ((q - x_pos) + (x_pos + nx - 1) % nx) * ny + y

    def near(k):
        return q * ny + (y + k + ny) % ny

    def piece(rows, k):
        return Wo.at[lanes(rows), lanes((y + k + ny) % ny)]

    def sideways(block):
        send(block, block, sO.at[3], rO.at[3], right, p)
        if nx > 2:
            send(block, block, sO.at[4], rO.at[4], left, p)

    def ring(t):
        if t > 0:
            wait(wout, rU.at[t - 1])
            wait(wout, rD.at[t - 1])
            sideways(piece(q, -t))
            sideways(piece(far, t))
            if t < reach:
                wait(wout, rU.at[reach + t - 1])
                wait(wout, rD.at[reach + t - 1])
                sideways(piece(far, -t))
                sideways(piece(q, t))
        else:
            sideways(piece(q, 0))
            sideways(piece(far, 0))
        if t < reach:
            send(piece(q, -t), piece(q, -t), sO.at[2], rU.at[t], near(1), p)
            send(piece(far, t), piece(far, t), sO.at[2], rD.at[t], near(-1), p)
        if t < reach - 1:
            send(piece(far, -t), piece(far, -t), sO.at[2], rU.at[reach + t], near(1), p)
            send(piece(q, t), piece(q, t), sO.at[2], rD.at[reach + t], near(-1), p)

    ring(0)
    loop(0, ns - 1, lambda k: send(Fs.at[away(k)], Fr.at[s], sV.at[0], rV.at[0], away(k), p))

    row = lax.broadcasted_iota(jnp.int32, (B, B), 0)
    col = lax.broadcasted_iota(jnp.int32, (B, B), 1)
    causal = col >= row
    per = ns // 8

    def toeplitz(i):
        for ch in range(cpd):
            def circulant(d):
                line = jnp.broadcast_to(Fr[pl.ds(d, 1), ch, :], (8, B))
                first = pltpu.roll(line, 0, 1, stride=1, stride_axis=0)
                rest = [pltpu.roll(first, 8 * k, 1) for k in range(1, B // 8)]
                return jnp.concatenate([first] + rest, axis=0)

            before = circulant(jnp.maximum(i * per - 1, 0))
            before = jnp.where(i == 0, jnp.zeros_like(before), before)

            def step(j, before):
                d = i * per + j
                now = circulant(d)
                T[ch, lanes(d), :] = jnp.where(causal, now, before).astype(BF16)
                return now

            lax.fori_loop(0, per, step, before)

    def halo_to(tb):
        return q * ny + tb + 1

    @pl.when(s == 0)
    def _():
        Hr[...] = jnp.zeros_like(Hr)

    def project(tb, own):
        wait(blocks(nzl), rC.at[tb])
        Ps[tb] = jnp.dot(F[tb], Wc[...], preferred_element_type=F32).astype(BF16)
        if own:
            Pr[y] = Ps[tb]
        else:
            send(Ps.at[tb], Pr.at[y], sP, rP, q * ny + tb, p)

        @pl.when(tb + 1 == y)
        def _():
            Hr[y] = Ps[tb, B - HALO:, :]

        @pl.when((tb + 1 != y) & (halo_to(tb) < ns))
        def _():
            send(Ps.at[tb, pl.ds(B - HALO, HALO), :], Hr.at[y], sH.at[tb], rH, halo_to(tb), p)

    relay(y)
    if reach > 1:
        ring(1)
    wait(Wb.at[pl.ds(0, nx - 1)], rW.at[1])
    wait(Wb.at[pl.ds(0, nx - 1)], rW.at[2])
    for k in range(np_):
        for stream in range(3):
            Wc[k * B:(k + 1) * B, stream * B:(stream + 1) * B] = Wb[k, stream]

    def main(i):
        relay(block_of(i))
        last_leg(block_of(i - 1))

        @pl.when(i == 2)
        def _():
            project(y, True)

        @pl.when(i > 2)
        def _():
            project(block_of(i - 2), False)

        for t in range(2, reach + 1):
            @pl.when(i == t - 1)
            def _(t=t):
                ring(t)

    if reach == 1:
        ring(1)
    loop(1, ny, main)
    last_leg(block_of(ny - 1))
    if ny > 2:
        project(block_of(ny - 2), False)
    else:
        project(y, True)
    project(block_of(ny - 1), False)

    sides = Wo.at[pl.ds(0, 2 * B)]
    wait(sides, rO.at[3])
    if nx > 2:
        wait(sides, rO.at[4])
        below = (q - x_pos) + (x_pos + nx - 1) % nx
        above = (far - x_pos % nx) + (x_pos + 1) % nx
        send(Wo.at[lanes(below)], Wo.at[lanes(below)], sO.at[5], rO.at[5], right, p)
        send(Wo.at[lanes(above)], Wo.at[lanes(above)], sO.at[5], rO.at[5], left, p)
    wait(Fr.at[pl.ds(0, ns - 1)], rV.at[0])
    loop(0, 6, toeplitz)

    wait(Pr.at[pl.ds(0, ny - 1)], rP)

    @pl.when(y > 0)
    def _():
        wait(Hr.at[pl.ds(0, ny - 1)], rH)

    @pl.when((y == 0) & (q > 0))
    def _():
        wait(Hr.at[pl.ds(0, ny)], rH)

    full = Pr[0].astype(F32)
    head = Hr[0].astype(F32)
    for k in range(1, ny):
        full = full + Pr[k].astype(F32)
        head = head + Hr[k].astype(F32)
    pad[HALO:] = full
    pad[:HALO] = head
    streams = []
    for stream in range(3):
        own = slice(stream * B, (stream + 1) * B)
        total = jnp.zeros((B, B), F32)
        for j in range(3):
            total = total + taps[stream, j:j + 1, :] * pad[HALO - j:HALO - j + B, own]
        streams.append(total)
    inner = streams[1] * streams[2]
    qi[0] = streams[0]
    qi[1] = inner

    turned = inner.T
    for k in range(cpd):
        Xs[:, k, :] = turned[k * ns:(k + 1) * ns]
    Xr[pl.ds(s, 1)] = Xs[pl.ds(s, 1)]
    loop(0, ns - 1, lambda k: send(Xs.at[away(k)], Xr.at[s], sV.at[1], rV.at[1], away(k), p))
    Xp[:ns] = jnp.zeros((ns, B), F32)
    loop(6, 8, toeplitz)

    wait(Xr.at[pl.ds(0, ns - 1)], rV.at[1])
    for ch in range(cpd):
        Xp[ns:] = Xr[:, ch, :]
        for d in range(ns):
            A[:, d * B:(d + 1) * B] = Xp[ns - d:2 * ns - d].astype(BF16)
        Ys[:, ch, :] = jnp.dot(A[...], T[ch], preferred_element_type=F32)
    Yr[pl.ds(s, 1)] = Ys[pl.ds(s, 1)]
    loop(0, ns - 1, lambda k: send(Ys.at[away(k)], Yr.at[s], sV.at[2], rV.at[2], away(k), p))
    wait(Yr.at[pl.ds(0, ns - 1)], rV.at[2])
    mix = jnp.concatenate([Yr[:, ch, :] for ch in range(cpd)], axis=0).T
    Gs[...] = (qi[0] * (mix + skip[...] * qi[1])).astype(BF16)

    gated = Gt.at[:, lanes(p)]
    for k in range(1, nzl):
        send(Gs, gated, sG, rG.at[0], s, ((zl + k) % nzl) * 2 + c)
    send(Gs, gated, sG, rG.at[1], s, mate)
    local(Gs, gated, loc.at[0])
    if nx > 2:
        wait(sides, rO.at[5])
    wait(Gs, loc.at[0])
    wait(Gt.at[:, pl.ds(0, (nzl - 1) * B)], rG.at[0])
    for k in range(1, nzl):
        other = Gt.at[:, lanes(((zl + k) % nzl) * 2 + c)]
        send(other, other, sG, rG.at[1], s, mate)
    wait(Gt.at[:, pl.ds(0, nzl * B)], rG.at[1])
    out[...] = jnp.dot(Gt[...], Wo[...], preferred_element_type=F32).astype(BF16)

    wait(F.at[pl.ds(0, ny - 1), :, pl.ds(0, B)], sF)
    wait(Wb.at[pl.ds(0, np_ - 1)], sW)
    if chain:
        @pl.when(end)
        def _():
            wait(F.at[:, :, pl.ds(0, 2 * B)], sZ)

        @pl.when(jnp.logical_not(end))
        def _():
            wait(F.at[:, :, pl.ds(0, 3 * B)], sZ)
            wait(F.at[:, :, pl.ds(0, B)], sE)
    else:
        wait(F.at[:, :, pl.ds(0, (nzl - 1) * B)], sZ)
    wait(F.at[:, :, pl.ds(0, nzl * B)], sC)
    wait(Pr.at[pl.ds(0, ny - 1)], sP)

    def halo_sent(tb):
        @pl.when((tb + 1 != y) & (halo_to(tb) < ns))
        def _():
            wait(Hr.at[0], sH.at[tb])

    loop(0, ny, halo_sent)
    for k in range(3):
        wait(Xs.at[pl.ds(0, ns - 1)], sV.at[k])
    wait(Gt.at[:, pl.ds(0, (2 * nzl - 1) * B)], sG)

    @pl.when(q != p)
    def _():
        wait(wout, sO.at[0])

    wait(wout, sO.at[1])
    wait(Wo.at[pl.ds(0, 2 * B), pl.ds(0, (ny - 1) * B)], sO.at[2])
    wait(sides, sO.at[3])
    if nx > 2:
        wait(sides, sO.at[4])
        wait(sides, sO.at[5])


def per_device(features, in_proj, short_taps, long_filter, skip_gain, out_proj):
    ns, np_ = lax.axis_size("seq"), lax.axis_size("tp")
    nx = np_ // 2
    ny = ns // np_
    cpd = B // ns
    dma = pltpu.SemaphoreType.DMA
    rows = pltpu.VMEM((ns, cpd, B), F32)
    return pl.pallas_call(
        functools.partial(kernel, ny, nx),
        out_shape=jax.ShapeDtypeStruct((B, ny * B), BF16),
        in_specs=[pl.BlockSpec(memory_space=pl.ANY)] * 6,
        out_specs=pl.BlockSpec(memory_space=pltpu.VMEM),
        scratch_shapes=[
            pltpu.VMEM((B, ny * B), BF16),
            pltpu.VMEM((3, B, B), BF16),
            pltpu.VMEM((3, 3, B), F32),
            pltpu.VMEM((B, B), F32),
            pltpu.VMEM((1, B), F32),
            pltpu.VMEM((B, B), BF16),
            pltpu.VMEM((ny, B, np_ * B), BF16),
            pltpu.VMEM((np_, 3, B, B), BF16),
            pltpu.VMEM((np_ * B, 3 * B), BF16),
            pltpu.VMEM((ny, B, 3 * B), BF16),
            pltpu.VMEM((ny, B, 3 * B), BF16),
            pltpu.VMEM((ny, HALO, 3 * B), BF16),
            pltpu.VMEM((HALO + B, 3 * B), F32),
            pltpu.VMEM((2, B, B), F32),
            rows, rows, rows, rows, rows, rows,
            pltpu.VMEM((2 * ns, B), F32),
            pltpu.VMEM((ns, ns * B), BF16),
            pltpu.VMEM((cpd, ns * B, B), BF16),
            pltpu.VMEM((B, B), BF16),
            pltpu.VMEM((B, np_ * B), BF16),
            pltpu.VMEM((np_ * B, ny * B), BF16),
            dma((6,)), dma((3,)),
            dma, dma((ny,)),
            dma, dma((3,)),
            dma, dma((ny,)),
            dma, dma((ny,)),
            dma, dma((ny,)),
            dma, dma,
            dma((ny,)), dma,
            dma((3,)), dma((3,)),
            dma, dma((2,)),
            dma((6,)), dma((6,)), dma((ny,)), dma((ny,)),
        ],
        compiler_params=pltpu.CompilerParams(
            collective_id=0, has_side_effects=True
        ),
        name="operator",
    )(features, in_proj, short_taps, long_filter, skip_gain.reshape(1, B), out_proj)


def solution(mesh):
    return jax.shard_map(
        per_device,
        mesh=mesh,
        in_specs=(
            P("seq", "tp"),
            P(None, "seq", "tp"),
            P(None, None, "tp"),
            P("seq", "tp"),
            P("tp"),
            P("tp", "seq"),
        ),
        out_specs=P("seq", "tp"),
        check_vma=False,
    )
```

```python
import functools

import jax
import jax.numpy as jnp
from jax import lax
from jax.experimental import pallas as pl
from jax.experimental.pallas import tpu as pltpu
from jax.sharding import PartitionSpec as P

B = 128
HALO = 16
BF16, F32 = jnp.bfloat16, jnp.float32


def lanes(i):
    return pl.ds(pl.multiple_of(i * B, B), B)


def kernel(
    ny, nx, feat_h, win_h, taps_h, filt_h, skip_h, wout_h, out,
    feat, win, taps, filt, skip, wout,
    F, Wb, Wc, Ps, Pr, Pf, Pe, Hs, Hr, pad, qi, Fs, Fr, Xs, Xr, Ys, Yr, Xp, A, T, Gs, Gt, Wo,
    arg, loc, sF, rF, sW, rW, sZ, rZ, sE, rE, sC, rC, sP, rP, rN, sH, rH, sV, rV, sG, rG, sO, rO, rU, rD, rR, rL,
):
    np_ = 2 * nx
    nq = 2 * nx
    nzl = np_ // 2
    ns = nq * ny
    cpd = B // ns
    s = lax.axis_index("seq")
    p = lax.axis_index("tp")
    q, y = s // ny, s % ny
    zl, c = p // 2, p % 2
    mate = p + 1 - 2 * c
    far = (q + nx) % nq
    chain = nzl == 4
    end = (zl == 0) | (zl == nzl - 1)

    def send(src, dst, ss, rs, sq, tp):
        pltpu.make_async_remote_copy(
            src_ref=src, dst_ref=dst, send_sem=ss, recv_sem=rs,
            device_id={"seq": sq, "tp": tp}, device_id_type=pl.DeviceIdType.MESH,
        ).start()

    def wait(ref, sem):
        pltpu.make_async_copy(ref, ref, sem).wait()

    def local(src, dst, sem):
        pltpu.make_async_copy(src, dst, sem).start()

    def loop(lo, hi, body):
        lax.fori_loop(lo, hi, lambda i, carry: (body(i), carry)[1], 0)

    def away(k):
        return (s + (k + ns // 3) % (ns - 1) + 1) % ns

    local(filt_h, filt, arg.at[0])
    local(feat_h, feat, arg.at[1])
    local(win_h, win, arg.at[2])
    local(wout_h, wout, arg.at[3])
    local(taps_h, taps, arg.at[4])
    local(skip_h, skip, arg.at[5])

    barrier = pltpu.get_barrier_semaphore()

    def greet(sq, tp):
        pl.semaphore_signal(
            barrier, inc=1, device_id={"seq": sq, "tp": tp}, device_id_type=pl.DeviceIdType.MESH
        )

    loop(0, ns - 1, lambda k: greet(away(k), p))
    greet(p * ny + y, far)

    @pl.when(q != p)
    def _():
        greet(p * ny + y, q)

    loop(1, np_, lambda k: greet(s, (p + k) % np_))

    wait(feat, arg.at[1])
    wait(win, arg.at[2])
    wait(wout, arg.at[3])
    local(feat.at[:, lanes(y)], F.at[y, :, lanes(p)], loc.at[0])
    local(win, Wb.at[q], loc.at[1])

    @pl.when(q == p)
    def _():
        local(wout, Wo.at[lanes(q), lanes(y)], loc.at[2])

    wait(filt, arg.at[0])
    turned = filt[...].T
    for k in range(cpd):
        Fs[:, k, :] = turned[k * ns:(k + 1) * ns]
    Fr[pl.ds(s, 1)] = Fs[pl.ds(s, 1)]
    wait(taps, arg.at[4])
    wait(skip, arg.at[5])
    wait(F.at[0, :, pl.ds(0, B)], loc.at[0])
    wait(win, loc.at[1])

    @pl.when(q == p)
    def _():
        wait(wout, loc.at[2])

    pl.semaphore_wait(barrier, ns + np_ - 1 + jnp.where(q == p, 0, 1))

    reach = ny // 2

    def distance(i):
        return reach - i // 2 if i % 2 == 0 else i // 2 + 1 - reach

    def near(k):
        return q * ny + (y + k + ny) % ny

    def block_of(i):
        return (y + distance(i) + ny) % ny

    def spread(i):
        to = block_of(i)
        send(feat.at[:, lanes(to)], F.at[y, :, lanes(p)], sF, rF.at[y], q * ny + to, p)

    def forward(tb):
        mine = F.at[tb, :, lanes(p)]
        for k in range(1, nzl):
            to = (zl + k) % nzl
            if chain:
                @pl.when((to - zl != 3) & (zl - to != 3))
                def _():
                    send(mine, mine, sZ, rZ.at[tb], s, to * 2 + c)
            else:
                send(mine, mine, sZ, rZ.at[tb], s, to * 2 + c)
        send(mine, mine, sC, rC.at[tb], s, mate)

    def pass_on(i):
        tb = block_of(i)
        wait(F.at[0, :, pl.ds(0, B)], rF.at[tb])
        forward(tb)

    def blocks(n):
        return F.at[0, :, pl.ds(0, n * B)]

    def relay(tb):
        def block(z):
            return F.at[tb, :, lanes(z * 2 + c)]

        if not chain:
            wait(blocks(nzl - 1), rZ.at[tb])
            for k in range(1, nzl):
                other = block((zl + k) % nzl)
                send(other, other, sC, rC.at[tb], s, mate)
            return

        @pl.when(end)
        def _():
            wait(blocks(2), rZ.at[tb])
            for k in range(1, 3):
                other = block(jnp.where(zl == 0, k, 3 - k))
                send(other, other, sC, rC.at[tb], s, mate)

        @pl.when(jnp.logical_not(end))
        def _():
            wait(blocks(3), rZ.at[tb])
            other = block(3 * (2 - zl))
            send(other, other, sE, rE.at[tb], s, 3 * (zl - 1) * 2 + c)
            for k in range(1, 4):
                other = block((zl + k) % 4)
                send(other, other, sC, rC.at[tb], s, mate)

    def last_leg(tb):
        if not chain:
            return

        @pl.when(end)
        def _():
            wait(blocks(1), rE.at[tb])
            other = F.at[tb, :, lanes((3 - zl) * 2 + c)]
            send(other, other, sC, rC.at[tb], s, mate)

    for i in range(ny - 1):
        spread(i)
    send(win, Wb.at[q], sW, rW.at[0], far * ny + y, p)
    forward(y)

    def weights(which, sem):
        def step(k):
            x = q % nx
            to = (q - x) + (x + k) % nx
            send(Wb.at[which], Wb.at[which], sW, sem, to * ny + y, p)

        loop(1, nx, step)

    weights(q, rW.at[1])

    @pl.when(q != p)
    def _():
        send(wout, Wo.at[lanes(p), lanes(y)], sO.at[0], rO.at[0], p * ny + y, q)

    send(wout, Wo.at[lanes(p), lanes(y)], sO.at[1], rO.at[1], ((p + nx) % nq) * ny + y, q)
    for i in range(ny - 1):
        pass_on(i)
    wait(Wb.at[0], rW.at[0])
    weights(far, rW.at[2])

    @pl.when(q != p)
    def _():
        wait(wout, rO.at[0])

    wait(wout, rO.at[1])
    x_pos = q % nx
    right = ((q - x_pos) + (x_pos + 1) % nx) * ny + y
    left = ((q - x_pos) + (x_pos + nx - 1) % nx) * ny + y

    def piece(rows, k):
        return Wo.at[lanes(rows), lanes((y + k + ny) % ny)]

    def sideways(block, t):
        send(block, block, sO.at[3], rR.at[t], right, p)
        if nx > 2:
            send(block, block, sO.at[4], rL.at[t], left, p)

    def columns(t):
        return (0,) if t == 0 else (t,) if t == reach else (-t, t)

    def across(t):
        got = Wo.at[pl.ds(0, B), pl.ds(0, 2 * len(columns(t)) * B)]
        wait(got, rR.at[t])
        if nx > 2:
            wait(got, rL.at[t])
            below = (q - x_pos) + (x_pos + nx - 1) % nx
            above = (far - x_pos) + (x_pos + 1) % nx
            for k in columns(t):
                send(piece(below, k), piece(below, k), sO.at[5], rO.at[5], right, p)
                send(piece(above, k), piece(above, k), sO.at[5], rO.at[5], left, p)

    def ring(t):
        if t > 0:
            wait(wout, rU.at[t - 1])
            wait(wout, rD.at[t - 1])
            sideways(piece(q, -t), t)
            sideways(piece(far, t), t)
            if t < reach:
                wait(wout, rU.at[reach + t - 1])
                wait(wout, rD.at[reach + t - 1])
                sideways(piece(far, -t), t)
                sideways(piece(q, t), t)
        else:
            sideways(piece(q, 0), 0)
            sideways(piece(far, 0), 0)
        if t < reach:
            send(piece(q, -t), piece(q, -t), sO.at[2], rU.at[t], near(1), p)
            send(piece(far, t), piece(far, t), sO.at[2], rD.at[t], near(-1), p)
        if t < reach - 1:
            send(piece(far, -t), piece(far, -t), sO.at[2], rU.at[reach + t], near(1), p)
            send(piece(q, t), piece(q, t), sO.at[2], rD.at[reach + t], near(-1), p)

    ring(0)
    loop(0, ns - 1, lambda k: send(Fs.at[away(k)], Fr.at[s], sV.at[0], rV.at[0], away(k), p))

    row = lax.broadcasted_iota(jnp.int32, (B, B), 0)
    col = lax.broadcasted_iota(jnp.int32, (B, B), 1)
    causal = col >= row
    per = ns // 8

    def toeplitz(i):
        for ch in range(cpd):
            def circulant(d):
                line = jnp.broadcast_to(Fr[pl.ds(d, 1), ch, :], (B, B))
                return pltpu.roll(line, 0, 1, stride=1, stride_axis=0)

            before = circulant(jnp.maximum(i * per - 1, 0))
            before = jnp.where(i == 0, jnp.zeros_like(before), before)

            def step(j, before):
                d = i * per + j
                now = circulant(d)
                T[ch, lanes(d), :] = jnp.where(causal, now, before).astype(BF16)
                return now

            lax.fori_loop(0, per, step, before, unroll=True)

    def halo_to(tb):
        return q * ny + tb + 1

    @pl.when(s == 0)
    def _():
        Hr[...] = jnp.zeros_like(Hr)

    def project(i):
        k, tb = distance(i), block_of(i)
        wait(blocks(nzl), rC.at[tb])
        total = jnp.dot(F[tb], Wc[...], preferred_element_type=F32)
        Hs[i] = total[B - HALO:].astype(BF16)

        @pl.when(tb + 1 == y)
        def _():
            Hr[y] = Hs[i]

        @pl.when((tb + 1 != y) & (halo_to(tb) < ns))
        def _():
            send(Hs.at[i], Hr.at[y], sH.at[i], rH, halo_to(tb), p)

        side = 0 if k > 0 else 1
        if k == 0:
            pad[HALO:] = total
            return
        if abs(k) < reach - side:
            wait(Ps.at[0], rP.at[i])
            total = total + Pr[i].astype(F32)
        to = near(1 - 2 * side)
        if abs(k) == 1:
            Pf[side] = total
            send(Pf.at[side], Pe.at[side], sP.at[i], rN.at[side], to, p)
        else:
            Ps[i] = total.astype(BF16)
            send(Ps.at[i], Pr.at[i + 2], sP.at[i], rP.at[i + 2], to, p)

    relay(y)
    wait(Wb.at[pl.ds(0, nx - 1)], rW.at[1])
    wait(Wb.at[pl.ds(0, nx - 1)], rW.at[2])
    for k in range(np_):
        for stream in range(3):
            Wc[k * B:(k + 1) * B, stream * B:(stream + 1) * B] = Wb[k, stream]

    last_leg(y)
    for i in range(ny - 1):
        relay(block_of(i))
        if i >= 1:
            last_leg(block_of(i - 1))
        if i >= 2:
            project(i - 2)
        if i % 2 == 1 and i // 2 + 1 <= reach:
            ring(i // 2 + 1)
            across(i // 2)
    last_leg(block_of(ny - 2))
    if ny > 2:
        project(ny - 3)
    project(ny - 2)
    ring(reach)
    across(reach - 1)
    project(ny - 1)
    wait(Fr.at[pl.ds(0, ns - 1)], rV.at[0])
    loop(0, 8, toeplitz)
    across(reach)

    full = pad[HALO:]
    for side in range(2 if ny > 2 else 1):
        wait(Pe.at[0], rN.at[side])
        full = full + Pe[side]

    @pl.when(y > 0)
    def _():
        wait(Hr.at[pl.ds(0, ny - 1)], rH)

    @pl.when((y == 0) & (q > 0))
    def _():
        wait(Hr.at[pl.ds(0, ny)], rH)

    head = Hr[0].astype(F32)
    for k in range(1, ny):
        head = head + Hr[k].astype(F32)
    pad[HALO:] = full
    pad[:HALO] = head
    streams = []
    for stream in range(3):
        own = slice(stream * B, (stream + 1) * B)
        total = jnp.zeros((B, B), F32)
        for j in range(3):
            total = total + taps[stream, j:j + 1, :] * pad[HALO - j:HALO - j + B, own]
        streams.append(total)
    inner = streams[1] * streams[2]
    qi[0] = streams[0]
    qi[1] = inner

    turned = inner.T
    for k in range(cpd):
        Xs[:, k, :] = turned[k * ns:(k + 1) * ns]
    Xr[pl.ds(s, 1)] = Xs[pl.ds(s, 1)]
    loop(0, ns - 1, lambda k: send(Xs.at[away(k)], Xr.at[s], sV.at[1], rV.at[1], away(k), p))
    Xp[:ns] = jnp.zeros((ns, B), F32)

    wait(Xr.at[pl.ds(0, ns - 1)], rV.at[1])
    for ch in range(cpd):
        Xp[ns:] = Xr[:, ch, :]
        for d in range(ns):
            A[:, d * B:(d + 1) * B] = Xp[ns - d:2 * ns - d].astype(BF16)
        Ys[:, ch, :] = jnp.dot(A[...], T[ch], preferred_element_type=F32)
    Yr[pl.ds(s, 1)] = Ys[pl.ds(s, 1)]
    loop(0, ns - 1, lambda k: send(Ys.at[away(k)], Yr.at[s], sV.at[2], rV.at[2], away(k), p))
    wait(Yr.at[pl.ds(0, ns - 1)], rV.at[2])
    mix = jnp.concatenate([Yr[:, ch, :] for ch in range(cpd)], axis=0).T
    Gs[...] = (qi[0] * (mix + skip[...] * qi[1])).astype(BF16)

    gated = Gt.at[:, lanes(p)]
    for k in range(1, nzl):
        send(Gs, gated, sG, rG.at[0], s, ((zl + k) % nzl) * 2 + c)
    send(Gs, gated, sG, rG.at[1], s, mate)
    local(Gs, gated, loc.at[0])
    if nx > 2:
        wait(Wo.at[pl.ds(0, 2 * B)], rO.at[5])
    wait(Gs, loc.at[0])
    wait(Gt.at[:, pl.ds(0, (nzl - 1) * B)], rG.at[0])
    for k in range(1, nzl):
        other = Gt.at[:, lanes(((zl + k) % nzl) * 2 + c)]
        send(other, other, sG, rG.at[1], s, mate)
    wait(Gt.at[:, pl.ds(0, nzl * B)], rG.at[1])
    out[...] = jnp.dot(Gt[...], Wo[...], preferred_element_type=F32).astype(BF16)

    wait(F.at[pl.ds(0, ny - 1), :, pl.ds(0, B)], sF)
    wait(Wb.at[pl.ds(0, np_ - 1)], sW)
    if chain:
        @pl.when(end)
        def _():
            wait(F.at[:, :, pl.ds(0, 2 * B)], sZ)

        @pl.when(jnp.logical_not(end))
        def _():
            wait(F.at[:, :, pl.ds(0, 3 * B)], sZ)
            wait(F.at[:, :, pl.ds(0, B)], sE)
    else:
        wait(F.at[:, :, pl.ds(0, (nzl - 1) * B)], sZ)
    wait(F.at[:, :, pl.ds(0, nzl * B)], sC)
    for i in range(ny):
        tb = block_of(i)

        @pl.when((tb + 1 != y) & (halo_to(tb) < ns))
        def _(i=i):
            wait(Hr.at[0], sH.at[i])

        if distance(i) != 0:
            wait(Pe.at[0] if abs(distance(i)) == 1 else Ps.at[0], sP.at[i])

    for k in range(3):
        wait(Xs.at[pl.ds(0, ns - 1)], sV.at[k])
    wait(Gt.at[:, pl.ds(0, (2 * nzl - 1) * B)], sG)

    @pl.when(q != p)
    def _():
        wait(wout, sO.at[0])

    wait(wout, sO.at[1])
    wait(Wo.at[pl.ds(0, 2 * B), pl.ds(0, (ny - 1) * B)], sO.at[2])
    sides = Wo.at[pl.ds(0, 2 * B)]
    wait(sides, sO.at[3])
    if nx > 2:
        wait(sides, sO.at[4])
        wait(sides, sO.at[5])


def per_device(features, in_proj, short_taps, long_filter, skip_gain, out_proj):
    ns, np_ = lax.axis_size("seq"), lax.axis_size("tp")
    nx = np_ // 2
    ny = ns // np_
    cpd = B // ns
    dma = pltpu.SemaphoreType.DMA
    rows = pltpu.VMEM((ns, cpd, B), F32)
    return pl.pallas_call(
        functools.partial(kernel, ny, nx),
        out_shape=jax.ShapeDtypeStruct((B, ny * B), BF16),
        in_specs=[pl.BlockSpec(memory_space=pl.ANY)] * 6,
        out_specs=pl.BlockSpec(memory_space=pltpu.VMEM),
        scratch_shapes=[
            pltpu.VMEM((B, ny * B), BF16),
            pltpu.VMEM((3, B, B), BF16),
            pltpu.VMEM((3, 3, B), F32),
            pltpu.VMEM((B, B), F32),
            pltpu.VMEM((1, B), F32),
            pltpu.VMEM((B, B), BF16),
            pltpu.VMEM((ny, B, np_ * B), BF16),
            pltpu.VMEM((np_, 3, B, B), BF16),
            pltpu.VMEM((np_ * B, 3 * B), BF16),
            pltpu.VMEM((ny, B, 3 * B), BF16),
            pltpu.VMEM((ny, B, 3 * B), BF16),
            pltpu.VMEM((2, B, 3 * B), F32),
            pltpu.VMEM((2, B, 3 * B), F32),
            pltpu.VMEM((ny, HALO, 3 * B), BF16),
            pltpu.VMEM((ny, HALO, 3 * B), BF16),
            pltpu.VMEM((HALO + B, 3 * B), F32),
            pltpu.VMEM((2, B, B), F32),
            rows, rows, rows, rows, rows, rows,
            pltpu.VMEM((2 * ns, B), F32),
            pltpu.VMEM((ns, ns * B), BF16),
            pltpu.VMEM((cpd, ns * B, B), BF16),
            pltpu.VMEM((B, B), BF16),
            pltpu.VMEM((B, np_ * B), BF16),
            pltpu.VMEM((np_ * B, ny * B), BF16),
            dma((6,)), dma((3,)),
            dma, dma((ny,)),
            dma, dma((3,)),
            dma, dma((ny,)),
            dma, dma((ny,)),
            dma, dma((ny,)),
            dma((ny,)), dma((ny,)), dma((2,)),
            dma((ny,)), dma,
            dma((3,)), dma((3,)),
            dma, dma((2,)),
            dma((6,)), dma((6,)), dma((ny,)), dma((ny,)), dma((ny,)), dma((ny,)),
        ],
        compiler_params=pltpu.CompilerParams(
            collective_id=0, has_side_effects=True
        ),
        name="operator",
    )(features, in_proj, short_taps, long_filter, skip_gain.reshape(1, B), out_proj)


def solution(mesh):
    return jax.shard_map(
        per_device,
        mesh=mesh,
        in_specs=(
            P("seq", "tp"),
            P(None, "seq", "tp"),
            P(None, None, "tp"),
            P("seq", "tp"),
            P("tp"),
            P("tp", "seq"),
        ),
        out_specs=P("seq", "tp"),
        check_vma=False,
    )
```

```python
import functools

import jax
import jax.numpy as jnp
from jax import lax
from jax.experimental import pallas as pl
from jax.experimental.pallas import tpu as pltpu
from jax.sharding import PartitionSpec as P

B = 128
HALO = 16
BF16, F32 = jnp.bfloat16, jnp.float32


def lanes(i):
    return pl.ds(pl.multiple_of(i * B, B), B)


def kernel(
    ny, nx, feat_h, win_h, taps_h, filt_h, skip_h, wout_h, out,
    feat, win, taps, filt, skip, wout,
    F, Wb, Wc, Ps, Pr, Pf, Pe, Hs, Hr, pad, qi, Fs, Fr, Xs, Xr, Ys, Yr, Xp, A, T, Gs, Gt, Wo,
    arg, loc, sF, rF, sW, rW, sZ, rZ, sE, rE, sC, rC, sP, rP, rN, sH, rH, sV, rV, sG, rG, sO, rO, rU, rD, rR, rL, round_y, round_x,
):
    np_ = 2 * nx
    nq = 2 * nx
    nzl = np_ // 2
    ns = nq * ny
    cpd = B // ns
    s = lax.axis_index("seq")
    p = lax.axis_index("tp")
    q, y = s // ny, s % ny
    zl, c = p // 2, p % 2
    mate = p + 1 - 2 * c
    far = (q + nx) % nq
    chain = nzl == 4
    end = (zl == 0) | (zl == nzl - 1)

    def send(src, dst, ss, rs, sq, tp):
        pltpu.make_async_remote_copy(
            src_ref=src, dst_ref=dst, send_sem=ss, recv_sem=rs,
            device_id={"seq": sq, "tp": tp}, device_id_type=pl.DeviceIdType.MESH,
        ).start()

    def wait(ref, sem):
        pltpu.make_async_copy(ref, ref, sem).wait()

    def local(src, dst, sem):
        pltpu.make_async_copy(src, dst, sem).start()

    def loop(lo, hi, body):
        lax.fori_loop(lo, hi, lambda i, carry: (body(i), carry)[1], 0)

    def away(k):
        return (s + (k + ns // 3) % (ns - 1) + 1) % ns

    local(filt_h, filt, arg.at[0])
    local(feat_h, feat, arg.at[1])
    local(win_h, win, arg.at[2])
    local(wout_h, wout, arg.at[3])
    local(taps_h, taps, arg.at[4])
    local(skip_h, skip, arg.at[5])

    barrier = pltpu.get_barrier_semaphore()

    def greet(sq, tp):
        pl.semaphore_signal(
            barrier, inc=1, device_id={"seq": sq, "tp": tp}, device_id_type=pl.DeviceIdType.MESH
        )

    x_pos = q % nx

    def x_line(k):
        return ((q - x_pos) + (x_pos + k) % nx) * ny + y

    def y_line(k):
        return q * ny + (y + k) % ny

    greet(p * ny + y, far)
    greet(far * ny + y, p)
    for k in range(1, ny):
        greet(y_line(k), p)
    for k in range(1, nx):
        greet(x_line(k), p)

    @pl.when(q != p)
    def _():
        greet(p * ny + y, q)

    for k in range(1, np_):
        greet(s, (p + k) % np_)

    wait(feat, arg.at[1])
    wait(win, arg.at[2])
    wait(wout, arg.at[3])
    local(feat.at[:, lanes(y)], F.at[y, :, lanes(p)], loc.at[0])
    local(win, Wb.at[q], loc.at[1])

    @pl.when(q == p)
    def _():
        local(wout, Wo.at[lanes(q), lanes(y)], loc.at[2])

    wait(filt, arg.at[0])
    turned = filt[...].T
    for k in range(cpd):
        Fs[:, k, :] = turned[k * ns:(k + 1) * ns]
    Fr[pl.ds(s, 1)] = Fs[pl.ds(s, 1)]
    wait(taps, arg.at[4])
    wait(skip, arg.at[5])
    wait(F.at[0, :, pl.ds(0, B)], loc.at[0])
    wait(win, loc.at[1])

    @pl.when(q == p)
    def _():
        wait(wout, loc.at[2])

    pl.semaphore_wait(barrier, 2 + ny - 1 + nx - 1 + np_ - 1 + jnp.where(q == p, 0, 1))

    def tell(sem, sq):
        pl.semaphore_signal(
            sem, inc=1, device_id={"seq": sq, "tp": p}, device_id_type=pl.DeviceIdType.MESH
        )

    reach = ny // 2

    def distance(i):
        return reach - i // 2 if i % 2 == 0 else i // 2 + 1 - reach

    def near(k):
        return q * ny + (y + k + ny) % ny

    def block_of(i):
        return (y + distance(i) + ny) % ny

    def spread(i):
        to = block_of(i)
        send(feat.at[:, lanes(to)], F.at[y, :, lanes(p)], sF, rF.at[y], q * ny + to, p)

    def forward(tb):
        mine = F.at[tb, :, lanes(p)]
        for k in range(1, nzl):
            to = (zl + k) % nzl
            if chain:
                @pl.when((to - zl != 3) & (zl - to != 3))
                def _():
                    send(mine, mine, sZ, rZ.at[tb], s, to * 2 + c)
            else:
                send(mine, mine, sZ, rZ.at[tb], s, to * 2 + c)
        send(mine, mine, sC, rC.at[tb], s, mate)

    def pass_on(i):
        tb = block_of(i)
        wait(F.at[0, :, pl.ds(0, B)], rF.at[tb])
        forward(tb)

    def blocks(n):
        return F.at[0, :, pl.ds(0, n * B)]

    def relay(tb):
        def block(z):
            return F.at[tb, :, lanes(z * 2 + c)]

        if not chain:
            wait(blocks(nzl - 1), rZ.at[tb])
            for k in range(1, nzl):
                other = block((zl + k) % nzl)
                send(other, other, sC, rC.at[tb], s, mate)
            return

        @pl.when(end)
        def _():
            wait(blocks(2), rZ.at[tb])
            for k in range(1, 3):
                other = block(jnp.where(zl == 0, k, 3 - k))
                send(other, other, sC, rC.at[tb], s, mate)

        @pl.when(jnp.logical_not(end))
        def _():
            wait(blocks(3), rZ.at[tb])
            other = block(3 * (2 - zl))
            send(other, other, sE, rE.at[tb], s, 3 * (zl - 1) * 2 + c)
            for k in range(1, 4):
                other = block((zl + k) % 4)
                send(other, other, sC, rC.at[tb], s, mate)

    def last_leg(tb):
        if not chain:
            return

        @pl.when(end)
        def _():
            wait(blocks(1), rE.at[tb])
            other = F.at[tb, :, lanes((3 - zl) * 2 + c)]
            send(other, other, sC, rC.at[tb], s, mate)

    for i in range(ny - 1):
        spread(i)
    send(win, Wb.at[q], sW, rW.at[0], far * ny + y, p)
    forward(y)

    def weights(which, sem):
        def step(k):
            x = q % nx
            to = (q - x) + (x + k) % nx
            send(Wb.at[which], Wb.at[which], sW, sem, to * ny + y, p)

        loop(1, nx, step)

    weights(q, rW.at[1])

    for k in range(1, ny):
        tell(round_y, y_line(k))

    @pl.when(q != p)
    def _():
        send(wout, Wo.at[lanes(p), lanes(y)], sO.at[0], rO.at[0], p * ny + y, q)

    send(wout, Wo.at[lanes(p), lanes(y)], sO.at[1], rO.at[1], ((p + nx) % nq) * ny + y, q)
    for i in range(ny - 1):
        pass_on(i)
    wait(Wb.at[0], rW.at[0])
    weights(far, rW.at[2])
    pl.semaphore_wait(round_y, ny - 1)
    for k in range(1, nx):
        tell(round_x, x_line(k))

    @pl.when(q != p)
    def _():
        wait(wout, rO.at[0])

    wait(wout, rO.at[1])
    right = ((q - x_pos) + (x_pos + 1) % nx) * ny + y
    left = ((q - x_pos) + (x_pos + nx - 1) % nx) * ny + y

    def piece(rows, k):
        return Wo.at[lanes(rows), lanes((y + k + ny) % ny)]

    def sideways(block, t):
        send(block, block, sO.at[3], rR.at[t], right, p)
        if nx > 2:
            send(block, block, sO.at[4], rL.at[t], left, p)

    def columns(t):
        return (0,) if t == 0 else (t,) if t == reach else (-t, t)

    def across(t):
        got = Wo.at[pl.ds(0, B), pl.ds(0, 2 * len(columns(t)) * B)]
        wait(got, rR.at[t])
        if nx > 2:
            wait(got, rL.at[t])
            below = (q - x_pos) + (x_pos + nx - 1) % nx
            above = (far - x_pos) + (x_pos + 1) % nx
            for k in columns(t):
                send(piece(below, k), piece(below, k), sO.at[5], rO.at[5], right, p)
                send(piece(above, k), piece(above, k), sO.at[5], rO.at[5], left, p)

    def ring(t):
        if t > 0:
            wait(wout, rU.at[t - 1])
            wait(wout, rD.at[t - 1])
            sideways(piece(q, -t), t)
            sideways(piece(far, t), t)
            if t < reach:
                wait(wout, rU.at[reach + t - 1])
                wait(wout, rD.at[reach + t - 1])
                sideways(piece(far, -t), t)
                sideways(piece(q, t), t)
        else:
            sideways(piece(q, 0), 0)
            sideways(piece(far, 0), 0)
        if t < reach:
            send(piece(q, -t), piece(q, -t), sO.at[2], rU.at[t], near(1), p)
            send(piece(far, t), piece(far, t), sO.at[2], rD.at[t], near(-1), p)
        if t < reach - 1:
            send(piece(far, -t), piece(far, -t), sO.at[2], rU.at[reach + t], near(1), p)
            send(piece(q, t), piece(q, t), sO.at[2], rD.at[reach + t], near(-1), p)

    ring(0)
    pl.semaphore_wait(round_x, nx - 1)
    loop(0, ns - 1, lambda k: send(Fs.at[away(k)], Fr.at[s], sV.at[0], rV.at[0], away(k), p))

    row = lax.broadcasted_iota(jnp.int32, (B, B), 0)
    col = lax.broadcasted_iota(jnp.int32, (B, B), 1)
    causal = col >= row
    per = ns // 8

    def toeplitz(i):
        for ch in range(cpd):
            def circulant(d):
                line = jnp.broadcast_to(Fr[pl.ds(d, 1), ch, :], (B, B))
                return pltpu.roll(line, 0, 1, stride=1, stride_axis=0)

            before = circulant(jnp.maximum(i * per - 1, 0))
            before = jnp.where(i == 0, jnp.zeros_like(before), before)

            def step(j, before):
                d = i * per + j
                now = circulant(d)
                T[ch, lanes(d), :] = jnp.where(causal, now, before).astype(BF16)
                return now

            lax.fori_loop(0, per, step, before, unroll=True)

    def halo_to(tb):
        return q * ny + tb + 1

    @pl.when(s == 0)
    def _():
        Hr[...] = jnp.zeros_like(Hr)

    def project(i):
        k, tb = distance(i), block_of(i)
        wait(blocks(nzl), rC.at[tb])
        total = jnp.dot(F[tb], Wc[...], preferred_element_type=F32)
        Hs[i] = total[B - HALO:].astype(BF16)

        @pl.when(tb + 1 == y)
        def _():
            Hr[y] = Hs[i]

        @pl.when((tb + 1 != y) & (halo_to(tb) < ns))
        def _():
            send(Hs.at[i], Hr.at[y], sH.at[i], rH, halo_to(tb), p)

        side = 0 if k > 0 else 1
        if k == 0:
            pad[HALO:] = total
            return
        if abs(k) < reach - side:
            wait(Ps.at[0], rP.at[i])
            total = total + Pr[i].astype(F32)
        to = near(1 - 2 * side)
        if abs(k) == 1:
            Pf[side] = total
            send(Pf.at[side], Pe.at[side], sP.at[i], rN.at[side], to, p)
        else:
            Ps[i] = total.astype(BF16)
            send(Ps.at[i], Pr.at[i + 2], sP.at[i], rP.at[i + 2], to, p)

    relay(y)
    wait(Wb.at[pl.ds(0, nx - 1)], rW.at[1])
    wait(Wb.at[pl.ds(0, nx - 1)], rW.at[2])
    for k in range(np_):
        for stream in range(3):
            Wc[k * B:(k + 1) * B, stream * B:(stream + 1) * B] = Wb[k, stream]

    last_leg(y)
    for i in range(ny - 1):
        relay(block_of(i))
        if i >= 1:
            last_leg(block_of(i - 1))
            project(i - 1)
        if i % 2 == 1 and i // 2 + 1 <= reach:
            ring(i // 2 + 1)
            across(i // 2)
    last_leg(block_of(ny - 2))
    project(ny - 2)
    ring(reach)
    across(reach - 1)
    project(ny - 1)
    wait(Fr.at[pl.ds(0, ns - 1)], rV.at[0])
    loop(0, 8, toeplitz)
    across(reach)

    full = pad[HALO:]
    for side in range(2 if ny > 2 else 1):
        wait(Pe.at[0], rN.at[side])
        full = full + Pe[side]

    @pl.when(y > 0)
    def _():
        wait(Hr.at[pl.ds(0, ny - 1)], rH)

    @pl.when((y == 0) & (q > 0))
    def _():
        wait(Hr.at[pl.ds(0, ny)], rH)

    head = Hr[0].astype(F32)
    for k in range(1, ny):
        head = head + Hr[k].astype(F32)
    pad[HALO:] = full
    pad[:HALO] = head
    streams = []
    for stream in range(3):
        own = slice(stream * B, (stream + 1) * B)
        total = jnp.zeros((B, B), F32)
        for j in range(3):
            total = total + taps[stream, j:j + 1, :] * pad[HALO - j:HALO - j + B, own]
        streams.append(total)
    inner = streams[1] * streams[2]
    qi[0] = streams[0]
    qi[1] = inner

    turned = inner.T
    for k in range(cpd):
        Xs[:, k, :] = turned[k * ns:(k + 1) * ns]
    Xr[pl.ds(s, 1)] = Xs[pl.ds(s, 1)]
    loop(0, ns - 1, lambda k: send(Xs.at[away(k)], Xr.at[s], sV.at[1], rV.at[1], away(k), p))
    Xp[:ns] = jnp.zeros((ns, B), F32)

    wait(Xr.at[pl.ds(0, ns - 1)], rV.at[1])
    for ch in range(cpd):
        Xp[ns:] = Xr[:, ch, :]
        for d in range(ns):
            A[:, d * B:(d + 1) * B] = Xp[ns - d:2 * ns - d].astype(BF16)
        Ys[:, ch, :] = jnp.dot(A[...], T[ch], preferred_element_type=F32)
    Yr[pl.ds(s, 1)] = Ys[pl.ds(s, 1)]
    loop(0, ns - 1, lambda k: send(Ys.at[away(k)], Yr.at[s], sV.at[2], rV.at[2], away(k), p))
    wait(Yr.at[pl.ds(0, ns - 1)], rV.at[2])
    mix = jnp.concatenate([Yr[:, ch, :] for ch in range(cpd)], axis=0).T
    Gs[...] = (qi[0] * (mix + skip[...] * qi[1])).astype(BF16)

    gated = Gt.at[:, lanes(p)]
    for k in range(1, nzl):
        send(Gs, gated, sG, rG.at[nzl - k], s, ((zl + k) % nzl) * 2 + c)
    send(Gs, gated, sG, rG.at[0], s, mate)
    local(Gs, gated, loc.at[0])
    if nx > 2:
        wait(Wo.at[pl.ds(0, 2 * B)], rO.at[5])
    wait(Gs, loc.at[0])
    for k in sorted(range(1, nzl), key=lambda k: min(k, nzl - k)):
        other = Gt.at[:, lanes(((zl + k) % nzl) * 2 + c)]
        wait(Gs, rG.at[k])
        send(other, other, sG, rG.at[0], s, mate)
    wait(Gt.at[:, pl.ds(0, nzl * B)], rG.at[0])
    out[...] = jnp.dot(Gt[...], Wo[...], preferred_element_type=F32).astype(BF16)

    wait(F.at[pl.ds(0, ny - 1), :, pl.ds(0, B)], sF)
    wait(Wb.at[pl.ds(0, np_ - 1)], sW)
    if chain:
        @pl.when(end)
        def _():
            wait(F.at[:, :, pl.ds(0, 2 * B)], sZ)

        @pl.when(jnp.logical_not(end))
        def _():
            wait(F.at[:, :, pl.ds(0, 3 * B)], sZ)
            wait(F.at[:, :, pl.ds(0, B)], sE)
    else:
        wait(F.at[:, :, pl.ds(0, (nzl - 1) * B)], sZ)
    wait(F.at[:, :, pl.ds(0, nzl * B)], sC)
    for i in range(ny):
        tb = block_of(i)

        @pl.when((tb + 1 != y) & (halo_to(tb) < ns))
        def _(i=i):
            wait(Hr.at[0], sH.at[i])

        if distance(i) != 0:
            wait(Pe.at[0] if abs(distance(i)) == 1 else Ps.at[0], sP.at[i])

    for k in range(3):
        wait(Xs.at[pl.ds(0, ns - 1)], sV.at[k])
    wait(Gt.at[:, pl.ds(0, (2 * nzl - 1) * B)], sG)

    @pl.when(q != p)
    def _():
        wait(wout, sO.at[0])

    wait(wout, sO.at[1])
    wait(Wo.at[pl.ds(0, 2 * B), pl.ds(0, (ny - 1) * B)], sO.at[2])
    sides = Wo.at[pl.ds(0, 2 * B)]
    wait(sides, sO.at[3])
    if nx > 2:
        wait(sides, sO.at[4])
        wait(sides, sO.at[5])


def per_device(features, in_proj, short_taps, long_filter, skip_gain, out_proj):
    ns, np_ = lax.axis_size("seq"), lax.axis_size("tp")
    nx = np_ // 2
    ny = ns // np_
    cpd = B // ns
    dma = pltpu.SemaphoreType.DMA
    rows = pltpu.VMEM((ns, cpd, B), F32)
    return pl.pallas_call(
        functools.partial(kernel, ny, nx),
        out_shape=jax.ShapeDtypeStruct((B, ny * B), BF16),
        in_specs=[pl.BlockSpec(memory_space=pl.ANY)] * 6,
        out_specs=pl.BlockSpec(memory_space=pltpu.VMEM),
        scratch_shapes=[
            pltpu.VMEM((B, ny * B), BF16),
            pltpu.VMEM((3, B, B), BF16),
            pltpu.VMEM((3, 3, B), F32),
            pltpu.VMEM((B, B), F32),
            pltpu.VMEM((1, B), F32),
            pltpu.VMEM((B, B), BF16),
            pltpu.VMEM((ny, B, np_ * B), BF16),
            pltpu.VMEM((np_, 3, B, B), BF16),
            pltpu.VMEM((np_ * B, 3 * B), BF16),
            pltpu.VMEM((ny, B, 3 * B), BF16),
            pltpu.VMEM((ny, B, 3 * B), BF16),
            pltpu.VMEM((2, B, 3 * B), F32),
            pltpu.VMEM((2, B, 3 * B), F32),
            pltpu.VMEM((ny, HALO, 3 * B), BF16),
            pltpu.VMEM((ny, HALO, 3 * B), BF16),
            pltpu.VMEM((HALO + B, 3 * B), F32),
            pltpu.VMEM((2, B, B), F32),
            rows, rows, rows, rows, rows, rows,
            pltpu.VMEM((2 * ns, B), F32),
            pltpu.VMEM((ns, ns * B), BF16),
            pltpu.VMEM((cpd, ns * B, B), BF16),
            pltpu.VMEM((B, B), BF16),
            pltpu.VMEM((B, np_ * B), BF16),
            pltpu.VMEM((np_ * B, ny * B), BF16),
            dma((6,)), dma((3,)),
            dma, dma((ny,)),
            dma, dma((3,)),
            dma, dma((ny,)),
            dma, dma((ny,)),
            dma, dma((ny,)),
            dma((ny,)), dma((ny,)), dma((2,)),
            dma((ny,)), dma,
            dma((3,)), dma((3,)),
            dma, dma((max(2, np_ // 2),)),
            dma((6,)), dma((6,)), dma((ny,)), dma((ny,)), dma((ny,)), dma((ny,)),
            pltpu.SemaphoreType.REGULAR, pltpu.SemaphoreType.REGULAR,
        ],
        compiler_params=pltpu.CompilerParams(
            collective_id=0, has_side_effects=True
        ),
        name="operator",
    )(features, in_proj, short_taps, long_filter, skip_gain.reshape(1, B), out_proj)


def solution(mesh):
    return jax.shard_map(
        per_device,
        mesh=mesh,
        in_specs=(
            P("seq", "tp"),
            P(None, "seq", "tp"),
            P(None, None, "tp"),
            P("seq", "tp"),
            P("tp"),
            P("tp", "seq"),
        ),
        out_specs=P("seq", "tp"),
        check_vma=False,
    )
```

```python
import functools

import jax
import jax.numpy as jnp
from jax import lax
from jax.experimental import pallas as pl
from jax.experimental.pallas import tpu as pltpu
from jax.sharding import PartitionSpec as P

B = 128
HALO = 16
BF16, F32 = jnp.bfloat16, jnp.float32


def lanes(i):
    return pl.ds(pl.multiple_of(i * B, B), B)


def kernel(
    ny, nx, feat_h, win_h, taps_h, filt_h, skip_h, wout_h, out,
    feat, win, taps, filt, skip, wout,
    F, Wb, Wc, Ps, Pr, Pf, Pe, Hs, Hr, pad, qi, Fs, Fr, Xs, Xr, Ys, Yr, Xp, A, T, Gs, Gt, Wo,
    arg, loc, sF, rF, sW, rW, sZ, rZ, sE, rE, sC, rC, sP, rP, rN, sH, rH, sV, rV, sG, rG, sO, rO, rU, rD, rR, rL, round_y, round_x,
):
    np_ = 2 * nx
    nq = 2 * nx
    nzl = np_ // 2
    ns = nq * ny
    cpd = B // ns
    s = lax.axis_index("seq")
    p = lax.axis_index("tp")
    q, y = s // ny, s % ny
    zl, c = p // 2, p % 2
    mate = p + 1 - 2 * c
    far = (q + nx) % nq
    chain = nzl == 4
    end = (zl == 0) | (zl == nzl - 1)

    def send(src, dst, ss, rs, sq, tp):
        pltpu.make_async_remote_copy(
            src_ref=src, dst_ref=dst, send_sem=ss, recv_sem=rs,
            device_id={"seq": sq, "tp": tp}, device_id_type=pl.DeviceIdType.MESH,
        ).start()

    def wait(ref, sem):
        pltpu.make_async_copy(ref, ref, sem).wait()

    def local(src, dst, sem):
        pltpu.make_async_copy(src, dst, sem).start()

    def loop(lo, hi, body):
        lax.fori_loop(lo, hi, lambda i, carry: (body(i), carry)[1], 0)

    def away(k):
        return lax.rem(s + lax.rem(k + ns // 3, ns - 1) + 1, ns)

    local(filt_h, filt, arg.at[0])
    local(feat_h, feat, arg.at[1])
    local(win_h, win, arg.at[2])
    local(wout_h, wout, arg.at[3])
    local(taps_h, taps, arg.at[4])
    local(skip_h, skip, arg.at[5])

    barrier = pltpu.get_barrier_semaphore()

    def greet(sq, tp):
        pl.semaphore_signal(
            barrier, inc=1, device_id={"seq": sq, "tp": tp}, device_id_type=pl.DeviceIdType.MESH
        )

    x_pos = q % nx

    def x_line(k):
        return ((q - x_pos) + (x_pos + k) % nx) * ny + y

    def y_line(k):
        return q * ny + (y + k) % ny

    greet(p * ny + y, far)
    greet(far * ny + y, p)
    for k in range(1, ny):
        greet(y_line(k), p)
    for k in range(1, nx):
        greet(x_line(k), p)

    @pl.when(q != p)
    def _():
        greet(p * ny + y, q)

    for k in range(1, np_):
        greet(s, (p + k) % np_)

    wait(feat, arg.at[1])
    wait(win, arg.at[2])
    wait(wout, arg.at[3])
    local(feat.at[:, lanes(y)], F.at[y, :, lanes(p)], loc.at[0])
    local(win, Wb.at[q], loc.at[1])

    @pl.when(q == p)
    def _():
        local(wout, Wo.at[lanes(q), lanes(y)], loc.at[2])

    pl.semaphore_wait(barrier, 2 + ny - 1 + nx - 1 + np_ - 1 + jnp.where(q == p, 0, 1))

    def tell(sem, sq):
        pl.semaphore_signal(
            sem, inc=1, device_id={"seq": sq, "tp": p}, device_id_type=pl.DeviceIdType.MESH
        )

    reach = ny // 2

    def distance(i):
        return reach - i // 2 if i % 2 == 0 else i // 2 + 1 - reach

    def near(k):
        return q * ny + (y + k + ny) % ny

    def block_of(i):
        return (y + distance(i) + ny) % ny

    def spread(i):
        to = block_of(i)
        send(feat.at[:, lanes(to)], F.at[y, :, lanes(p)], sF, rF.at[y], q * ny + to, p)

    def forward(tb):
        mine = F.at[tb, :, lanes(p)]
        for k in range(1, nzl):
            to = (zl + k) % nzl
            if chain:
                @pl.when((to - zl != 3) & (zl - to != 3))
                def _():
                    send(mine, mine, sZ, rZ.at[tb], s, to * 2 + c)
            else:
                send(mine, mine, sZ, rZ.at[tb], s, to * 2 + c)
        send(mine, mine, sC, rC.at[tb], s, mate)

    def pass_on(i):
        tb = block_of(i)
        wait(F.at[0, :, pl.ds(0, B)], rF.at[tb])
        forward(tb)

    def blocks(n):
        return F.at[0, :, pl.ds(0, n * B)]

    def relay(tb):
        def block(z):
            return F.at[tb, :, lanes(z * 2 + c)]

        if not chain:
            wait(blocks(nzl - 1), rZ.at[tb])
            for k in range(1, nzl):
                other = block((zl + k) % nzl)
                send(other, other, sC, rC.at[tb], s, mate)
            return

        @pl.when(end)
        def _():
            wait(blocks(2), rZ.at[tb])
            for k in range(1, 3):
                other = block(jnp.where(zl == 0, k, 3 - k))
                send(other, other, sC, rC.at[tb], s, mate)

        @pl.when(jnp.logical_not(end))
        def _():
            wait(blocks(3), rZ.at[tb])
            other = block(3 * (2 - zl))
            send(other, other, sE, rE.at[tb], s, 3 * (zl - 1) * 2 + c)
            for k in range(1, 4):
                other = block((zl + k) % 4)
                send(other, other, sC, rC.at[tb], s, mate)

    def last_leg(tb):
        if not chain:
            return

        @pl.when(end)
        def _():
            wait(blocks(1), rE.at[tb])
            other = F.at[tb, :, lanes((3 - zl) * 2 + c)]
            send(other, other, sC, rC.at[tb], s, mate)

    for i in range(ny - 1):
        spread(i)
    send(win, Wb.at[q], sW, rW.at[0], far * ny + y, p)
    wait(F.at[0, :, pl.ds(0, B)], loc.at[0])
    forward(y)
    wait(win, loc.at[1])

    def weights(which, sem):
        def step(k):
            x = q % nx
            to = (q - x) + (x + k) % nx
            send(Wb.at[which], Wb.at[which], sW, sem, to * ny + y, p)

        loop(1, nx, step)

    weights(q, rW.at[1])

    for k in range(1, ny):
        tell(round_y, y_line(k))

    @pl.when(q != p)
    def _():
        send(wout, Wo.at[lanes(p), lanes(y)], sO.at[0], rO.at[0], p * ny + y, q)

    send(wout, Wo.at[lanes(p), lanes(y)], sO.at[1], rO.at[1], ((p + nx) % nq) * ny + y, q)
    for i in range(ny - 1):
        pass_on(i)
    wait(Wb.at[0], rW.at[0])
    weights(far, rW.at[2])
    pl.semaphore_wait(round_y, ny - 1)
    for k in range(1, nx):
        tell(round_x, x_line(k))

    @pl.when(q == p)
    def _():
        wait(wout, loc.at[2])

    @pl.when(q != p)
    def _():
        wait(wout, rO.at[0])

    wait(wout, rO.at[1])
    right = ((q - x_pos) + (x_pos + 1) % nx) * ny + y
    left = ((q - x_pos) + (x_pos + nx - 1) % nx) * ny + y

    def piece(rows, k):
        return Wo.at[lanes(rows), lanes((y + k + ny) % ny)]

    def sideways(block, t):
        send(block, block, sO.at[3], rR.at[t], right, p)
        if nx > 2:
            send(block, block, sO.at[4], rL.at[t], left, p)

    def columns(t):
        return (0,) if t == 0 else (t,) if t == reach else (-t, t)

    def across(t):
        got = Wo.at[pl.ds(0, B), pl.ds(0, 2 * len(columns(t)) * B)]
        wait(got, rR.at[t])
        if nx > 2:
            wait(got, rL.at[t])
            below = (q - x_pos) + (x_pos + nx - 1) % nx
            above = (far - x_pos) + (x_pos + 1) % nx
            for k in columns(t):
                send(piece(below, k), piece(below, k), sO.at[5], rO.at[5], right, p)
                send(piece(above, k), piece(above, k), sO.at[5], rO.at[5], left, p)

    def ring(t):
        if t > 0:
            wait(wout, rU.at[t - 1])
            wait(wout, rD.at[t - 1])
            sideways(piece(q, -t), t)
            sideways(piece(far, t), t)
            if t < reach:
                wait(wout, rU.at[reach + t - 1])
                wait(wout, rD.at[reach + t - 1])
                sideways(piece(far, -t), t)
                sideways(piece(q, t), t)
        else:
            sideways(piece(q, 0), 0)
            sideways(piece(far, 0), 0)
        if t < reach:
            send(piece(q, -t), piece(q, -t), sO.at[2], rU.at[t], near(1), p)
            send(piece(far, t), piece(far, t), sO.at[2], rD.at[t], near(-1), p)
        if t < reach - 1:
            send(piece(far, -t), piece(far, -t), sO.at[2], rU.at[reach + t], near(1), p)
            send(piece(q, t), piece(q, t), sO.at[2], rD.at[reach + t], near(-1), p)

    ring(0)
    wait(filt, arg.at[0])
    turned = filt[...].T
    for k in range(cpd):
        Fs[:, k, :] = turned[k * ns:(k + 1) * ns]
    Fr[pl.ds(s, 1)] = Fs[pl.ds(s, 1)]
    wait(taps, arg.at[4])
    wait(skip, arg.at[5])
    pl.semaphore_wait(round_x, nx - 1)
    loop(0, ns - 1, lambda k: send(Fs.at[away(k)], Fr.at[s], sV.at[0], rV.at[0], away(k), p))

    row = lax.broadcasted_iota(jnp.int32, (B, B), 0)
    col = lax.broadcasted_iota(jnp.int32, (B, B), 1)
    causal = col >= row
    per = ns // 8

    def toeplitz(i):
        for ch in range(cpd):
            def circulant(d):
                line = jnp.broadcast_to(Fr[pl.ds(d, 1), ch, :], (B, B))
                return pltpu.roll(line, 0, 1, stride=1, stride_axis=0)

            before = circulant(jnp.maximum(i * per - 1, 0))
            before = jnp.where(i == 0, jnp.zeros_like(before), before)

            def step(j, before):
                d = i * per + j
                now = circulant(d)
                T[ch, lanes(d), :] = jnp.where(causal, now, before).astype(BF16)
                return now

            lax.fori_loop(0, per, step, before, unroll=True)

    def halo_to(tb):
        return q * ny + tb + 1

    @pl.when(s == 0)
    def _():
        Hr[...] = jnp.zeros_like(Hr)

    def project(i):
        k, tb = distance(i), block_of(i)
        wait(blocks(nzl), rC.at[tb])
        total = jnp.dot(F[tb], Wc[...], preferred_element_type=F32)
        Hs[i] = total[B - HALO:].astype(BF16)

        @pl.when(tb + 1 == y)
        def _():
            Hr[y] = Hs[i]

        @pl.when((tb + 1 != y) & (halo_to(tb) < ns))
        def _():
            send(Hs.at[i], Hr.at[y], sH.at[i], rH, halo_to(tb), p)

        side = 0 if k > 0 else 1
        if k == 0:
            pad[HALO:] = total
            return
        if abs(k) < reach - side:
            wait(Ps.at[0], rP.at[i])
            total = total + Pr[i].astype(F32)
        to = near(1 - 2 * side)
        if abs(k) == 1:
            Pf[side] = total
            send(Pf.at[side], Pe.at[side], sP.at[i], rN.at[side], to, p)
        else:
            Ps[i] = total.astype(BF16)
            send(Ps.at[i], Pr.at[i + 2], sP.at[i], rP.at[i + 2], to, p)

    relay(y)
    wait(Wb.at[pl.ds(0, nx - 1)], rW.at[1])
    wait(Wb.at[pl.ds(0, nx - 1)], rW.at[2])
    for k in range(np_):
        for stream in range(3):
            Wc[k * B:(k + 1) * B, stream * B:(stream + 1) * B] = Wb[k, stream]

    last_leg(y)
    for i in range(ny - 1):
        relay(block_of(i))
        if i >= 1:
            last_leg(block_of(i - 1))
            project(i - 1)
        if i == 1 and reach > 2:
            ring(1)
        if i == 4:
            ring(2)
            across(0)
    last_leg(block_of(ny - 2))
    project(ny - 2)
    early = 2 if reach > 2 else 0
    if early:
        ring(3)
        across(1)
    project(ny - 1)
    wait(Fr.at[pl.ds(0, ns - 1)], rV.at[0])
    loop(0, 8, toeplitz)
    for t in range(early + 2 if early else 1, reach + 1):
        ring(t)
    if early:
        across(2)

    full = pad[HALO:]
    for side in range(2 if ny > 2 else 1):
        wait(Pe.at[0], rN.at[side])
        full = full + Pe[side]

    @pl.when(y > 0)
    def _():
        wait(Hr.at[pl.ds(0, ny - 1)], rH)

    @pl.when((y == 0) & (q > 0))
    def _():
        wait(Hr.at[pl.ds(0, ny)], rH)

    head = Hr[0].astype(F32)
    for k in range(1, ny):
        head = head + Hr[k].astype(F32)
    pad[HALO:] = full
    pad[:HALO] = head
    streams = []
    for stream in range(3):
        own = slice(stream * B, (stream + 1) * B)
        total = jnp.zeros((B, B), F32)
        for j in range(3):
            total = total + taps[stream, j:j + 1, :] * pad[HALO - j:HALO - j + B, own]
        streams.append(total)
    inner = streams[1] * streams[2]
    qi[0] = streams[0]
    qi[1] = inner

    turned = inner.T
    for k in range(cpd):
        Xs[:, k, :] = turned[k * ns:(k + 1) * ns]
    Xr[pl.ds(s, 1)] = Xs[pl.ds(s, 1)]
    loop(0, ns - 1, lambda k: send(Xs.at[away(k)], Xr.at[s], sV.at[1], rV.at[1], away(k), p))
    Xp[:ns] = jnp.zeros((ns, B), F32)
    for t in range(early + 1 if early else 0, reach + 1):
        across(t)

    wait(Xr.at[pl.ds(0, ns - 1)], rV.at[1])
    for ch in range(cpd):
        Xp[ns:] = Xr[:, ch, :]
        for d in range(ns):
            A[:, d * B:(d + 1) * B] = Xp[ns - d:2 * ns - d].astype(BF16)
        Ys[:, ch, :] = jnp.dot(A[...], T[ch], preferred_element_type=F32)
    Yr[pl.ds(s, 1)] = Ys[pl.ds(s, 1)]
    loop(0, ns - 1, lambda k: send(Ys.at[away(k)], Yr.at[s], sV.at[2], rV.at[2], away(k), p))
    wait(Yr.at[pl.ds(0, ns - 1)], rV.at[2])
    mix = jnp.concatenate([Yr[:, ch, :] for ch in range(cpd)], axis=0).T
    Gs[...] = (qi[0] * (mix + skip[...] * qi[1])).astype(BF16)

    gated = Gt.at[:, lanes(p)]
    for k in range(1, nzl):
        send(Gs, gated, sG, rG.at[nzl - k], s, ((zl + k) % nzl) * 2 + c)
    send(Gs, gated, sG, rG.at[0], s, mate)
    local(Gs, gated, loc.at[0])
    if nx > 2:
        wait(Wo.at[pl.ds(0, 2 * B)], rO.at[5])
    wait(Gs, loc.at[0])
    for k in sorted(range(1, nzl), key=lambda k: min(k, nzl - k)):
        other = Gt.at[:, lanes(((zl + k) % nzl) * 2 + c)]
        wait(Gs, rG.at[k])
        send(other, other, sG, rG.at[0], s, mate)
    wait(Gt.at[:, pl.ds(0, nzl * B)], rG.at[0])
    out[...] = jnp.dot(Gt[...], Wo[...], preferred_element_type=F32).astype(BF16)

    wait(F.at[pl.ds(0, ny - 1), :, pl.ds(0, B)], sF)
    wait(Wb.at[pl.ds(0, np_ - 1)], sW)
    if chain:
        @pl.when(end)
        def _():
            wait(F.at[:, :, pl.ds(0, 2 * B)], sZ)

        @pl.when(jnp.logical_not(end))
        def _():
            wait(F.at[:, :, pl.ds(0, 3 * B)], sZ)
            wait(F.at[:, :, pl.ds(0, B)], sE)
    else:
        wait(F.at[:, :, pl.ds(0, (nzl - 1) * B)], sZ)
    wait(F.at[:, :, pl.ds(0, nzl * B)], sC)
    for i in range(ny):
        tb = block_of(i)

        @pl.when((tb + 1 != y) & (halo_to(tb) < ns))
        def _(i=i):
            wait(Hr.at[0], sH.at[i])

        if distance(i) != 0:
            wait(Pe.at[0] if abs(distance(i)) == 1 else Ps.at[0], sP.at[i])

    for k in range(3):
        wait(Xs.at[pl.ds(0, ns - 1)], sV.at[k])
    wait(Gt.at[:, pl.ds(0, (2 * nzl - 1) * B)], sG)

    @pl.when(q != p)
    def _():
        wait(wout, sO.at[0])

    wait(wout, sO.at[1])
    wait(Wo.at[pl.ds(0, 2 * B), pl.ds(0, (ny - 1) * B)], sO.at[2])
    sides = Wo.at[pl.ds(0, 2 * B)]
    wait(sides, sO.at[3])
    if nx > 2:
        wait(sides, sO.at[4])
        wait(sides, sO.at[5])


def per_device(features, in_proj, short_taps, long_filter, skip_gain, out_proj):
    ns, np_ = lax.axis_size("seq"), lax.axis_size("tp")
    nx = np_ // 2
    ny = ns // np_
    cpd = B // ns
    dma = pltpu.SemaphoreType.DMA
    rows = pltpu.VMEM((ns, cpd, B), F32)
    return pl.pallas_call(
        functools.partial(kernel, ny, nx),
        out_shape=jax.ShapeDtypeStruct((B, ny * B), BF16),
        in_specs=[pl.BlockSpec(memory_space=pl.ANY)] * 6,
        out_specs=pl.BlockSpec(memory_space=pltpu.VMEM),
        scratch_shapes=[
            pltpu.VMEM((B, ny * B), BF16),
            pltpu.VMEM((3, B, B), BF16),
            pltpu.VMEM((3, 3, B), F32),
            pltpu.VMEM((B, B), F32),
            pltpu.VMEM((1, B), F32),
            pltpu.VMEM((B, B), BF16),
            pltpu.VMEM((ny, B, np_ * B), BF16),
            pltpu.VMEM((np_, 3, B, B), BF16),
            pltpu.VMEM((np_ * B, 3 * B), BF16),
            pltpu.VMEM((ny, B, 3 * B), BF16),
            pltpu.VMEM((ny, B, 3 * B), BF16),
            pltpu.VMEM((2, B, 3 * B), F32),
            pltpu.VMEM((2, B, 3 * B), F32),
            pltpu.VMEM((ny, HALO, 3 * B), BF16),
            pltpu.VMEM((ny, HALO, 3 * B), BF16),
            pltpu.VMEM((HALO + B, 3 * B), F32),
            pltpu.VMEM((2, B, B), F32),
            rows, rows, rows, rows, rows, rows,
            pltpu.VMEM((2 * ns, B), F32),
            pltpu.VMEM((ns, ns * B), BF16),
            pltpu.VMEM((cpd, ns * B, B), BF16),
            pltpu.VMEM((B, B), BF16),
            pltpu.VMEM((B, np_ * B), BF16),
            pltpu.VMEM((np_ * B, ny * B), BF16),
            dma((6,)), dma((3,)),
            dma, dma((ny,)),
            dma, dma((3,)),
            dma, dma((ny,)),
            dma, dma((ny,)),
            dma, dma((ny,)),
            dma((ny,)), dma((ny,)), dma((2,)),
            dma((ny,)), dma,
            dma((3,)), dma((3,)),
            dma, dma((max(2, np_ // 2),)),
            dma((6,)), dma((6,)), dma((ny,)), dma((ny,)), dma((ny,)), dma((ny,)),
            pltpu.SemaphoreType.REGULAR, pltpu.SemaphoreType.REGULAR,
        ],
        compiler_params=pltpu.CompilerParams(
            collective_id=0, has_side_effects=True
        ),
        name="operator",
    )(features, in_proj, short_taps, long_filter, skip_gain.reshape(1, B), out_proj)


def solution(mesh):
    return jax.shard_map(
        per_device,
        mesh=mesh,
        in_specs=(
            P("seq", "tp"),
            P(None, "seq", "tp"),
            P(None, None, "tp"),
            P("seq", "tp"),
            P("tp"),
            P("tp", "seq"),
        ),
        out_specs=P("seq", "tp"),
        check_vma=False,
    )
```

```python
import functools

import jax
import jax.numpy as jnp
from jax import lax
from jax.experimental import pallas as pl
from jax.experimental.pallas import tpu as pltpu
from jax.sharding import PartitionSpec as P

B = 128
HALO = 16
BF16, F32 = jnp.bfloat16, jnp.float32


def lanes(i):
    return pl.ds(pl.multiple_of(i * B, B), B)


def kernel(
    ny, nx, feat_h, win_h, taps_h, filt_h, skip_h, wout_h, out,
    feat, win, taps, filt, skip, wout,
    F, Wb, Wc, Ps, Pr, Pf, Pe, Hs, Hr, pad, qi, Fs, Fr, Xs, Xr, Ys, Yr, Xp, A, T, Gs, Gt, Wo,
    arg, loc, sF, rF, sW, rW, sZ, rZ, sE, rE, sC, rC, sP, rP, rN, sH, rH, sV, rV, sG, rG, sO, rO, rU, rD, rR, rL, round_y, round_x,
):
    np_ = 2 * nx
    nq = 2 * nx
    nzl = np_ // 2
    ns = nq * ny
    cpd = B // ns
    s = lax.axis_index("seq")
    p = lax.axis_index("tp")
    q, y = s // ny, s % ny
    zl, c = p // 2, p % 2
    mate = p + 1 - 2 * c
    far = (q + nx) % nq
    chain = nzl == 4
    end = (zl == 0) | (zl == nzl - 1)

    def send(src, dst, ss, rs, sq, tp):
        pltpu.make_async_remote_copy(
            src_ref=src, dst_ref=dst, send_sem=ss, recv_sem=rs,
            device_id={"seq": sq, "tp": tp}, device_id_type=pl.DeviceIdType.MESH,
        ).start()

    def wait(ref, sem):
        pltpu.make_async_copy(ref, ref, sem).wait()

    def local(src, dst, sem):
        pltpu.make_async_copy(src, dst, sem).start()

    def loop(lo, hi, body):
        lax.fori_loop(lo, hi, lambda i, carry: (body(i), carry)[1], 0)

    def away(k):
        return lax.rem(s + lax.rem(k + ns // 3, ns - 1) + 1, ns)

    local(filt_h, filt, arg.at[0])
    local(feat_h, feat, arg.at[1])
    local(win_h, win, arg.at[2])
    local(wout_h, wout, arg.at[3])
    local(taps_h, taps, arg.at[4])
    local(skip_h, skip, arg.at[5])

    barrier = pltpu.get_barrier_semaphore()

    def greet(sq, tp):
        pl.semaphore_signal(
            barrier, inc=1, device_id={"seq": sq, "tp": tp}, device_id_type=pl.DeviceIdType.MESH
        )

    x_pos = q % nx

    def x_line(k):
        return ((q - x_pos) + (x_pos + k) % nx) * ny + y

    def y_line(k):
        return q * ny + (y + k) % ny

    greet(p * ny + y, far)
    greet(far * ny + y, p)
    for k in range(1, ny):
        greet(y_line(k), p)
    for k in range(1, nx):
        greet(x_line(k), p)

    @pl.when(q != p)
    def _():
        greet(p * ny + y, q)

    for k in range(1, np_):
        greet(s, (p + k) % np_)

    wait(feat, arg.at[1])
    wait(win, arg.at[2])
    wait(wout, arg.at[3])
    local(feat.at[:, lanes(y)], F.at[y, :, lanes(p)], loc.at[0])
    local(win, Wb.at[q], loc.at[1])

    @pl.when(q == p)
    def _():
        local(wout, Wo.at[lanes(q), lanes(y)], loc.at[2])

    pl.semaphore_wait(barrier, 2 + ny - 1 + nx - 1 + np_ - 1 + jnp.where(q == p, 0, 1))

    def tell(sem, sq):
        pl.semaphore_signal(
            sem, inc=1, device_id={"seq": sq, "tp": p}, device_id_type=pl.DeviceIdType.MESH
        )

    reach = ny // 2

    def distance(i):
        return reach - i // 2 if i % 2 == 0 else i // 2 + 1 - reach

    def near(k):
        return q * ny + (y + k + ny) % ny

    def block_of(i):
        return (y + distance(i) + ny) % ny

    def spread(i):
        to = block_of(i)
        send(feat.at[:, lanes(to)], F.at[y, :, lanes(p)], sF, rF.at[y], q * ny + to, p)

    def forward(tb):
        mine = F.at[tb, :, lanes(p)]
        for k in range(1, nzl):
            to = (zl + k) % nzl
            if chain:
                @pl.when((to - zl != 3) & (zl - to != 3))
                def _():
                    send(mine, mine, sZ, rZ.at[tb], s, to * 2 + c)
            else:
                send(mine, mine, sZ, rZ.at[tb], s, to * 2 + c)
        send(mine, mine, sC, rC.at[tb], s, mate)

    def pass_on(i):
        tb = block_of(i)
        wait(F.at[0, :, pl.ds(0, B)], rF.at[tb])
        forward(tb)

    def blocks(n):
        return F.at[0, :, pl.ds(0, n * B)]

    def relay(tb):
        def block(z):
            return F.at[tb, :, lanes(z * 2 + c)]

        if not chain:
            wait(blocks(nzl - 1), rZ.at[tb])
            for k in range(1, nzl):
                other = block((zl + k) % nzl)
                send(other, other, sC, rC.at[tb], s, mate)
            return

        @pl.when(end)
        def _():
            wait(blocks(2), rZ.at[tb])
            for k in range(1, 3):
                other = block(jnp.where(zl == 0, k, 3 - k))
                send(other, other, sC, rC.at[tb], s, mate)

        @pl.when(jnp.logical_not(end))
        def _():
            wait(blocks(3), rZ.at[tb])
            other = block(3 * (2 - zl))
            send(other, other, sE, rE.at[tb], s, 3 * (zl - 1) * 2 + c)
            for k in range(1, 4):
                other = block((zl + k) % 4)
                send(other, other, sC, rC.at[tb], s, mate)

    def last_leg(tb):
        if not chain:
            return

        @pl.when(end)
        def _():
            wait(blocks(1), rE.at[tb])
            other = F.at[tb, :, lanes((3 - zl) * 2 + c)]
            send(other, other, sC, rC.at[tb], s, mate)

    for i in range(ny - 1):
        spread(i)
    send(win, Wb.at[q], sW, rW.at[0], far * ny + y, p)
    wait(F.at[0, :, pl.ds(0, B)], loc.at[0])
    forward(y)
    wait(win, loc.at[1])

    def weights(which, sem):
        def step(k):
            x = q % nx
            to = (q - x) + (x + k) % nx
            send(Wb.at[which], Wb.at[which], sW, sem, to * ny + y, p)

        loop(1, nx, step)

    weights(q, rW.at[1])

    for k in range(1, ny):
        tell(round_y, y_line(k))

    @pl.when(q != p)
    def _():
        send(wout, Wo.at[lanes(p), lanes(y)], sO.at[0], rO.at[0], p * ny + y, q)

    send(wout, Wo.at[lanes(p), lanes(y)], sO.at[1], rO.at[1], ((p + nx) % nq) * ny + y, q)
    for i in range(ny - 1):
        pass_on(i)
    wait(Wb.at[0], rW.at[0])
    weights(far, rW.at[2])
    pl.semaphore_wait(round_y, ny - 1)
    for k in range(1, nx):
        tell(round_x, x_line(k))

    @pl.when(q == p)
    def _():
        wait(wout, loc.at[2])

    @pl.when(q != p)
    def _():
        wait(wout, rO.at[0])

    wait(wout, rO.at[1])
    right = ((q - x_pos) + (x_pos + 1) % nx) * ny + y
    left = ((q - x_pos) + (x_pos + nx - 1) % nx) * ny + y

    def piece(rows, k):
        return Wo.at[lanes(rows), lanes((y + k + ny) % ny)]

    def sideways(block, t):
        send(block, block, sO.at[3], rR.at[t], right, p)
        if nx > 2:
            send(block, block, sO.at[4], rL.at[t], left, p)

    def columns(t):
        return (0,) if t == 0 else (t,) if t == reach else (-t, t)

    def across(t):
        got = Wo.at[pl.ds(0, B), pl.ds(0, 2 * len(columns(t)) * B)]
        wait(got, rR.at[t])
        if nx > 2:
            wait(got, rL.at[t])
            below = (q - x_pos) + (x_pos + nx - 1) % nx
            above = (far - x_pos) + (x_pos + 1) % nx
            for k in columns(t):
                send(piece(below, k), piece(below, k), sO.at[5], rO.at[5], right, p)
                send(piece(above, k), piece(above, k), sO.at[5], rO.at[5], left, p)

    def ring(t):
        if t > 0:
            wait(wout, rU.at[t - 1])
            wait(wout, rD.at[t - 1])
            sideways(piece(q, -t), t)
            sideways(piece(far, t), t)
            if t < reach:
                wait(wout, rU.at[reach + t - 1])
                wait(wout, rD.at[reach + t - 1])
                sideways(piece(far, -t), t)
                sideways(piece(q, t), t)
        else:
            sideways(piece(q, 0), 0)
            sideways(piece(far, 0), 0)
        if t < reach:
            send(piece(q, -t), piece(q, -t), sO.at[2], rU.at[t], near(1), p)
            send(piece(far, t), piece(far, t), sO.at[2], rD.at[t], near(-1), p)
        if t < reach - 1:
            send(piece(far, -t), piece(far, -t), sO.at[2], rU.at[reach + t], near(1), p)
            send(piece(q, t), piece(q, t), sO.at[2], rD.at[reach + t], near(-1), p)

    ring(0)
    wait(filt, arg.at[0])
    turned = filt[...].T
    for k in range(cpd):
        Fs[:, k, :] = turned[k * ns:(k + 1) * ns]
    Fr[pl.ds(s, 1)] = Fs[pl.ds(s, 1)]
    wait(taps, arg.at[4])
    wait(skip, arg.at[5])
    pl.semaphore_wait(round_x, nx - 1)
    loop(0, ns - 1, lambda k: send(Fs.at[away(k)], Fr.at[s], sV.at[0], rV.at[0], away(k), p))

    row = lax.broadcasted_iota(jnp.int32, (B, B), 0)
    col = lax.broadcasted_iota(jnp.int32, (B, B), 1)
    causal = col >= row
    per = ns // 8

    def toeplitz(i):
        for ch in range(cpd):
            def circulant(d):
                line = jnp.broadcast_to(Fr[pl.ds(d, 1), ch, :], (B, B))
                return pltpu.roll(line, 0, 1, stride=1, stride_axis=0)

            before = circulant(jnp.maximum(i * per - 1, 0))
            before = jnp.where(i == 0, jnp.zeros_like(before), before)

            def step(j, before):
                d = i * per + j
                now = circulant(d)
                T[ch, lanes(d), :] = jnp.where(causal, now, before).astype(BF16)
                return now

            lax.fori_loop(0, per, step, before, unroll=True)

    def halo_to(tb):
        return q * ny + tb + 1

    @pl.when(s == 0)
    def _():
        Hr[...] = jnp.zeros_like(Hr)

    def project(i):
        k, tb = distance(i), block_of(i)
        wait(blocks(nzl), rC.at[tb])
        total = jnp.dot(F[tb], Wc[...], preferred_element_type=F32)
        Hs[i] = total[B - HALO:].astype(BF16)

        @pl.when(tb + 1 == y)
        def _():
            Hr[y] = Hs[i]

        @pl.when((tb + 1 != y) & (halo_to(tb) < ns))
        def _():
            send(Hs.at[i], Hr.at[y], sH.at[i], rH, halo_to(tb), p)

        side = 0 if k > 0 else 1
        if k == 0:
            pad[HALO:] = total
            return
        if abs(k) < reach - side:
            wait(Ps.at[0], rP.at[i])
            total = total + Pr[i].astype(F32)
        to = near(1 - 2 * side)
        if abs(k) == 1:
            Pf[side] = total
            send(Pf.at[side], Pe.at[side], sP.at[i], rN.at[side], to, p)
        else:
            Ps[i] = total.astype(BF16)
            send(Ps.at[i], Pr.at[i + 2], sP.at[i], rP.at[i + 2], to, p)

    relay(y)
    wait(Wb.at[pl.ds(0, nx - 1)], rW.at[1])
    wait(Wb.at[pl.ds(0, nx - 1)], rW.at[2])
    for k in range(np_):
        for stream in range(3):
            Wc[k * B:(k + 1) * B, stream * B:(stream + 1) * B] = Wb[k, stream]

    last_leg(y)
    for i in range(ny - 1):
        relay(block_of(i))
        if i >= 1:
            last_leg(block_of(i - 1))
            project(i - 1)
        if i == 1 and reach > 2:
            ring(1)
        if i == 4:
            ring(2)
            across(0)
    last_leg(block_of(ny - 2))
    project(ny - 2)
    early = 2 if reach > 2 else 0
    if early:
        ring(3)
        across(1)
    project(ny - 1)
    wait(Fr.at[pl.ds(0, ns - 1)], rV.at[0])
    loop(0, 8, toeplitz)

    full = pad[HALO:]
    for side in range(2 if ny > 2 else 1):
        wait(Pe.at[0], rN.at[side])
        full = full + Pe[side]

    @pl.when(y > 0)
    def _():
        wait(Hr.at[pl.ds(0, ny - 1)], rH)

    @pl.when((y == 0) & (q > 0))
    def _():
        wait(Hr.at[pl.ds(0, ny)], rH)

    head = Hr[0].astype(F32)
    for k in range(1, ny):
        head = head + Hr[k].astype(F32)
    pad[HALO:] = full
    pad[:HALO] = head
    streams = []
    for stream in range(3):
        own = slice(stream * B, (stream + 1) * B)
        total = jnp.zeros((B, B), F32)
        for j in range(3):
            total = total + taps[stream, j:j + 1, :] * pad[HALO - j:HALO - j + B, own]
        streams.append(total)
    inner = streams[1] * streams[2]
    qi[0] = streams[0]
    qi[1] = inner

    turned = inner.T
    for k in range(cpd):
        Xs[:, k, :] = turned[k * ns:(k + 1) * ns]
    Xr[pl.ds(s, 1)] = Xs[pl.ds(s, 1)]
    loop(0, ns - 1, lambda k: send(Xs.at[away(k)], Xr.at[s], sV.at[1], rV.at[1], away(k), p))
    Xp[:ns] = jnp.zeros((ns, B), F32)
    for t in range(early + 2 if early else 1, reach + 1):
        ring(t)
    for t in range(early, reach + 1):
        across(t)

    wait(Xr.at[pl.ds(0, ns - 1)], rV.at[1])
    for ch in range(cpd):
        Xp[ns:] = Xr[:, ch, :]
        for d in range(ns):
            A[:, d * B:(d + 1) * B] = Xp[ns - d:2 * ns - d].astype(BF16)
        Ys[:, ch, :] = jnp.dot(A[...], T[ch], preferred_element_type=F32)
    Yr[pl.ds(s, 1)] = Ys[pl.ds(s, 1)]
    loop(0, ns - 1, lambda k: send(Ys.at[away(k)], Yr.at[s], sV.at[2], rV.at[2], away(k), p))
    wait(Yr.at[pl.ds(0, ns - 1)], rV.at[2])
    mix = jnp.concatenate([Yr[:, ch, :] for ch in range(cpd)], axis=0).T
    Gs[...] = (qi[0] * (mix + skip[...] * qi[1])).astype(BF16)

    gated = Gt.at[:, lanes(p)]
    for k in range(1, nzl):
        send(Gs, gated, sG, rG.at[nzl - k], s, ((zl + k) % nzl) * 2 + c)
    send(Gs, gated, sG, rG.at[0], s, mate)
    local(Gs, gated, loc.at[0])
    if nx > 2:
        wait(Wo.at[pl.ds(0, 2 * B)], rO.at[5])
    wait(Gs, loc.at[0])
    for k in sorted(range(1, nzl), key=lambda k: min(k, nzl - k)):
        other = Gt.at[:, lanes(((zl + k) % nzl) * 2 + c)]
        wait(Gs, rG.at[k])
        send(other, other, sG, rG.at[0], s, mate)
    wait(Gt.at[:, pl.ds(0, nzl * B)], rG.at[0])
    out[...] = jnp.dot(Gt[...], Wo[...], preferred_element_type=F32).astype(BF16)

    wait(F.at[pl.ds(0, ny - 1), :, pl.ds(0, B)], sF)
    wait(Wb.at[pl.ds(0, np_ - 1)], sW)
    if chain:
        @pl.when(end)
        def _():
            wait(F.at[:, :, pl.ds(0, 2 * B)], sZ)

        @pl.when(jnp.logical_not(end))
        def _():
            wait(F.at[:, :, pl.ds(0, 3 * B)], sZ)
            wait(F.at[:, :, pl.ds(0, B)], sE)
    else:
        wait(F.at[:, :, pl.ds(0, (nzl - 1) * B)], sZ)
    wait(F.at[:, :, pl.ds(0, nzl * B)], sC)
    for i in range(ny):
        tb = block_of(i)

        @pl.when((tb + 1 != y) & (halo_to(tb) < ns))
        def _(i=i):
            wait(Hr.at[0], sH.at[i])

        if distance(i) != 0:
            wait(Pe.at[0] if abs(distance(i)) == 1 else Ps.at[0], sP.at[i])

    for k in range(3):
        wait(Xs.at[pl.ds(0, ns - 1)], sV.at[k])
    wait(Gt.at[:, pl.ds(0, (2 * nzl - 1) * B)], sG)

    @pl.when(q != p)
    def _():
        wait(wout, sO.at[0])

    wait(wout, sO.at[1])
    wait(Wo.at[pl.ds(0, 2 * B), pl.ds(0, (ny - 1) * B)], sO.at[2])
    sides = Wo.at[pl.ds(0, 2 * B)]
    wait(sides, sO.at[3])
    if nx > 2:
        wait(sides, sO.at[4])
        wait(sides, sO.at[5])


def per_device(features, in_proj, short_taps, long_filter, skip_gain, out_proj):
    ns, np_ = lax.axis_size("seq"), lax.axis_size("tp")
    nx = np_ // 2
    ny = ns // np_
    cpd = B // ns
    dma = pltpu.SemaphoreType.DMA
    rows = pltpu.VMEM((ns, cpd, B), F32)
    return pl.pallas_call(
        functools.partial(kernel, ny, nx),
        out_shape=jax.ShapeDtypeStruct((B, ny * B), BF16),
        in_specs=[pl.BlockSpec(memory_space=pl.ANY)] * 6,
        out_specs=pl.BlockSpec(memory_space=pltpu.VMEM),
        scratch_shapes=[
            pltpu.VMEM((B, ny * B), BF16),
            pltpu.VMEM((3, B, B), BF16),
            pltpu.VMEM((3, 3, B), F32),
            pltpu.VMEM((B, B), F32),
            pltpu.VMEM((1, B), F32),
            pltpu.VMEM((B, B), BF16),
            pltpu.VMEM((ny, B, np_ * B), BF16),
            pltpu.VMEM((np_, 3, B, B), BF16),
            pltpu.VMEM((np_ * B, 3 * B), BF16),
            pltpu.VMEM((ny, B, 3 * B), BF16),
            pltpu.VMEM((ny, B, 3 * B), BF16),
            pltpu.VMEM((2, B, 3 * B), F32),
            pltpu.VMEM((2, B, 3 * B), F32),
            pltpu.VMEM((ny, HALO, 3 * B), BF16),
            pltpu.VMEM((ny, HALO, 3 * B), BF16),
            pltpu.VMEM((HALO + B, 3 * B), F32),
            pltpu.VMEM((2, B, B), F32),
            rows, rows, rows, rows, rows, rows,
            pltpu.VMEM((2 * ns, B), F32),
            pltpu.VMEM((ns, ns * B), BF16),
            pltpu.VMEM((cpd, ns * B, B), BF16),
            pltpu.VMEM((B, B), BF16),
            pltpu.VMEM((B, np_ * B), BF16),
            pltpu.VMEM((np_ * B, ny * B), BF16),
            dma((6,)), dma((3,)),
            dma, dma((ny,)),
            dma, dma((3,)),
            dma, dma((ny,)),
            dma, dma((ny,)),
            dma, dma((ny,)),
            dma((ny,)), dma((ny,)), dma((2,)),
            dma((ny,)), dma,
            dma((3,)), dma((3,)),
            dma, dma((max(2, np_ // 2),)),
            dma((6,)), dma((6,)), dma((ny,)), dma((ny,)), dma((ny,)), dma((ny,)),
            pltpu.SemaphoreType.REGULAR, pltpu.SemaphoreType.REGULAR,
        ],
        compiler_params=pltpu.CompilerParams(
            collective_id=0, has_side_effects=True
        ),
        name="operator",
    )(features, in_proj, short_taps, long_filter, skip_gain.reshape(1, B), out_proj)


def solution(mesh):
    return jax.shard_map(
        per_device,
        mesh=mesh,
        in_specs=(
            P("seq", "tp"),
            P(None, "seq", "tp"),
            P(None, None, "tp"),
            P("seq", "tp"),
            P("tp"),
            P("tp", "seq"),
        ),
        out_specs=P("seq", "tp"),
        check_vma=False,
    )
```

```python
import functools

import jax
import jax.numpy as jnp
from jax import lax
from jax.experimental import pallas as pl
from jax.experimental.pallas import tpu as pltpu
from jax.sharding import PartitionSpec as P

B = 128
HALO = 16
BF16, F32 = jnp.bfloat16, jnp.float32


def lanes(i):
    return pl.ds(pl.multiple_of(i * B, B), B)


def kernel(
    ny, nx, feat_h, win_h, taps_h, filt_h, skip_h, wout_h, out,
    feat, win, taps, filt, skip, wout,
    F, Wb, Wc, Ps, Pr, Pf, Pe, Hs, Hr, pad, qi, Fs, Fr, Xs, Xr, Ys, Yr, Xp, A, T, Gs, Gt, Wo,
    arg, loc, sF, rF, sW, rW, sZ, rZ, sE, rE, sC, rC, sP, rP, rN, sH, rH, sV, rV, sG, rG, sO, rO, rU, rD, rR, rL, round_y, round_x,
):
    np_ = 2 * nx
    nq = 2 * nx
    nzl = np_ // 2
    ns = nq * ny
    cpd = B // ns
    s = lax.axis_index("seq")
    p = lax.axis_index("tp")
    q, y = s // ny, s % ny
    zl, c = p // 2, p % 2
    mate = p + 1 - 2 * c
    far = (q + nx) % nq
    chain = nzl == 4
    end = (zl == 0) | (zl == nzl - 1)

    def send(src, dst, ss, rs, sq, tp):
        pltpu.make_async_remote_copy(
            src_ref=src, dst_ref=dst, send_sem=ss, recv_sem=rs,
            device_id={"seq": sq, "tp": tp}, device_id_type=pl.DeviceIdType.MESH,
        ).start()

    def wait(ref, sem):
        pltpu.make_async_copy(ref, ref, sem).wait()

    def local(src, dst, sem):
        pltpu.make_async_copy(src, dst, sem).start()

    def loop(lo, hi, body):
        unroll = 7 if hi == ns - 1 else 1
        lax.fori_loop(lo, hi, lambda i, carry: (body(i), carry)[1], 0, unroll=unroll)

    def away(k):
        return lax.rem(s + lax.rem(k + ns // 3, ns - 1) + 1, ns)

    local(filt_h, filt, arg.at[0])
    local(feat_h, feat, arg.at[1])
    local(win_h, win, arg.at[2])
    local(wout_h, wout, arg.at[3])
    local(taps_h, taps, arg.at[4])
    local(skip_h, skip, arg.at[5])

    barrier = pltpu.get_barrier_semaphore()

    def greet(sq, tp):
        pl.semaphore_signal(
            barrier, inc=1, device_id={"seq": sq, "tp": tp}, device_id_type=pl.DeviceIdType.MESH
        )

    x_pos = q % nx

    def x_line(k):
        return ((q - x_pos) + (x_pos + k) % nx) * ny + y

    def y_line(k):
        return q * ny + (y + k) % ny

    greet(p * ny + y, far)
    greet(far * ny + y, p)
    for k in range(1, ny):
        greet(y_line(k), p)
    for k in range(1, nx):
        greet(x_line(k), p)

    @pl.when(q != p)
    def _():
        greet(p * ny + y, q)

    for k in range(1, np_):
        greet(s, (p + k) % np_)

    wait(feat, arg.at[1])
    wait(win, arg.at[2])
    wait(wout, arg.at[3])
    local(feat.at[:, lanes(y)], F.at[y, :, lanes(p)], loc.at[0])
    local(win, Wb.at[q], loc.at[1])

    @pl.when(q == p)
    def _():
        local(wout, Wo.at[lanes(q), lanes(y)], loc.at[2])

    wait(filt, arg.at[0])
    turned = filt[...].T
    for k in range(cpd):
        Fs[:, k, :] = turned[k * ns:(k + 1) * ns]
    Fr[pl.ds(s, 1)] = Fs[pl.ds(s, 1)]
    wait(taps, arg.at[4])
    wait(skip, arg.at[5])
    wait(F.at[0, :, pl.ds(0, B)], loc.at[0])
    wait(win, loc.at[1])

    @pl.when(q == p)
    def _():
        wait(wout, loc.at[2])

    pl.semaphore_wait(barrier, 2 + ny - 1 + nx - 1 + np_ - 1 + jnp.where(q == p, 0, 1))

    def tell(sem, sq):
        pl.semaphore_signal(
            sem, inc=1, device_id={"seq": sq, "tp": p}, device_id_type=pl.DeviceIdType.MESH
        )

    reach = ny // 2

    def distance(i):
        return reach - i // 2 if i % 2 == 0 else i // 2 + 1 - reach

    def near(k):
        return q * ny + (y + k + ny) % ny

    def block_of(i):
        return (y + distance(i) + ny) % ny

    def spread(i):
        to = block_of(i)
        send(feat.at[:, lanes(to)], F.at[y, :, lanes(p)], sF, rF.at[y], q * ny + to, p)

    def forward(tb):
        mine = F.at[tb, :, lanes(p)]
        for k in range(1, nzl):
            to = (zl + k) % nzl
            if chain:
                @pl.when((to - zl != 3) & (zl - to != 3))
                def _():
                    send(mine, mine, sZ, rZ.at[tb], s, to * 2 + c)
            else:
                send(mine, mine, sZ, rZ.at[tb], s, to * 2 + c)
        send(mine, mine, sC, rC.at[tb], s, mate)

    def pass_on(i):
        tb = block_of(i)
        wait(F.at[0, :, pl.ds(0, B)], rF.at[tb])
        forward(tb)

    def blocks(n):
        return F.at[0, :, pl.ds(0, n * B)]

    def relay(tb):
        def block(z):
            return F.at[tb, :, lanes(z * 2 + c)]

        if not chain:
            wait(blocks(nzl - 1), rZ.at[tb])
            for k in range(1, nzl):
                other = block((zl + k) % nzl)
                send(other, other, sC, rC.at[tb], s, mate)
            return

        @pl.when(end)
        def _():
            wait(blocks(2), rZ.at[tb])
            for k in range(1, 3):
                other = block(jnp.where(zl == 0, k, 3 - k))
                send(other, other, sC, rC.at[tb], s, mate)

        @pl.when(jnp.logical_not(end))
        def _():
            wait(blocks(3), rZ.at[tb])
            other = block(3 * (2 - zl))
            send(other, other, sE, rE.at[tb], s, 3 * (zl - 1) * 2 + c)
            for k in range(1, 4):
                other = block((zl + k) % 4)
                send(other, other, sC, rC.at[tb], s, mate)

    def last_leg(tb):
        if not chain:
            return

        @pl.when(end)
        def _():
            wait(blocks(1), rE.at[tb])
            other = F.at[tb, :, lanes((3 - zl) * 2 + c)]
            send(other, other, sC, rC.at[tb], s, mate)

    for i in range(ny - 1):
        spread(i)
    send(win, Wb.at[q], sW, rW.at[0], far * ny + y, p)
    forward(y)

    def weights(which, sem):
        def step(k):
            x = q % nx
            to = (q - x) + (x + k) % nx
            send(Wb.at[which], Wb.at[which], sW, sem, to * ny + y, p)

        loop(1, nx, step)

    weights(q, rW.at[1])

    for k in range(1, ny):
        tell(round_y, y_line(k))

    @pl.when(q != p)
    def _():
        send(wout, Wo.at[lanes(p), lanes(y)], sO.at[0], rO.at[0], p * ny + y, q)

    send(wout, Wo.at[lanes(p), lanes(y)], sO.at[1], rO.at[1], ((p + nx) % nq) * ny + y, q)
    for i in range(ny - 1):
        pass_on(i)
    wait(Wb.at[0], rW.at[0])
    weights(far, rW.at[2])
    pl.semaphore_wait(round_y, ny - 1)
    for k in range(1, nx):
        tell(round_x, x_line(k))

    @pl.when(q != p)
    def _():
        wait(wout, rO.at[0])

    wait(wout, rO.at[1])
    right = ((q - x_pos) + (x_pos + 1) % nx) * ny + y
    left = ((q - x_pos) + (x_pos + nx - 1) % nx) * ny + y

    def piece(rows, k):
        return Wo.at[lanes(rows), lanes((y + k + ny) % ny)]

    def sideways(block, t):
        send(block, block, sO.at[3], rR.at[t], right, p)
        if nx > 2:
            send(block, block, sO.at[4], rL.at[t], left, p)

    def columns(t):
        return (0,) if t == 0 else (t,) if t == reach else (-t, t)

    def across(t):
        got = Wo.at[pl.ds(0, B), pl.ds(0, 2 * len(columns(t)) * B)]
        wait(got, rR.at[t])
        if nx > 2:
            wait(got, rL.at[t])
            below = (q - x_pos) + (x_pos + nx - 1) % nx
            above = (far - x_pos) + (x_pos + 1) % nx
            for k in columns(t):
                send(piece(below, k), piece(below, k), sO.at[5], rO.at[5], right, p)
                send(piece(above, k), piece(above, k), sO.at[5], rO.at[5], left, p)

    def ring(t):
        if t > 0:
            wait(wout, rU.at[t - 1])
            wait(wout, rD.at[t - 1])
            sideways(piece(q, -t), t)
            sideways(piece(far, t), t)
            if t < reach:
                wait(wout, rU.at[reach + t - 1])
                wait(wout, rD.at[reach + t - 1])
                sideways(piece(far, -t), t)
                sideways(piece(q, t), t)
        else:
            sideways(piece(q, 0), 0)
            sideways(piece(far, 0), 0)
        if t < reach:
            send(piece(q, -t), piece(q, -t), sO.at[2], rU.at[t], near(1), p)
            send(piece(far, t), piece(far, t), sO.at[2], rD.at[t], near(-1), p)
        if t < reach - 1:
            send(piece(far, -t), piece(far, -t), sO.at[2], rU.at[reach + t], near(1), p)
            send(piece(q, t), piece(q, t), sO.at[2], rD.at[reach + t], near(-1), p)

    ring(0)
    pl.semaphore_wait(round_x, nx - 1)
    loop(0, ns - 1, lambda k: send(Fs.at[away(k)], Fr.at[s], sV.at[0], rV.at[0], away(k), p))

    row = lax.broadcasted_iota(jnp.int32, (B, B), 0)
    col = lax.broadcasted_iota(jnp.int32, (B, B), 1)
    causal = col >= row
    per = ns // 8

    def toeplitz(i):
        for ch in range(cpd):
            def circulant(d):
                line = jnp.broadcast_to(Fr[pl.ds(d, 1), ch, :], (B, B))
                return pltpu.roll(line, 0, 1, stride=1, stride_axis=0)

            before = circulant(jnp.maximum(i * per - 1, 0))
            before = jnp.where(i == 0, jnp.zeros_like(before), before)

            def step(j, before):
                d = i * per + j
                now = circulant(d)
                T[ch, lanes(d), :] = jnp.where(causal, now, before).astype(BF16)
                return now

            lax.fori_loop(0, per, step, before, unroll=True)

    def halo_to(tb):
        return q * ny + tb + 1

    @pl.when(s == 0)
    def _():
        Hr[...] = jnp.zeros_like(Hr)

    def project(i):
        k, tb = distance(i), block_of(i)
        wait(blocks(nzl), rC.at[tb])
        total = jnp.dot(F[tb], Wc[...], preferred_element_type=F32)
        Hs[i] = total[B - HALO:].astype(BF16)

        @pl.when(tb + 1 == y)
        def _():
            Hr[y] = Hs[i]

        @pl.when((tb + 1 != y) & (halo_to(tb) < ns))
        def _():
            send(Hs.at[i], Hr.at[y], sH.at[i], rH, halo_to(tb), p)

        side = 0 if k > 0 else 1
        if k == 0:
            pad[HALO:] = total
            return
        if abs(k) < reach - side:
            wait(Ps.at[0], rP.at[i])
            total = total + Pr[i].astype(F32)
        to = near(1 - 2 * side)
        if abs(k) == 1:
            Pf[side] = total
            send(Pf.at[side], Pe.at[side], sP.at[i], rN.at[side], to, p)
        else:
            Ps[i] = total.astype(BF16)
            send(Ps.at[i], Pr.at[i + 2], sP.at[i], rP.at[i + 2], to, p)

    relay(y)
    wait(Wb.at[pl.ds(0, nx - 1)], rW.at[1])
    wait(Wb.at[pl.ds(0, nx - 1)], rW.at[2])
    for k in range(np_):
        for stream in range(3):
            Wc[k * B:(k + 1) * B, stream * B:(stream + 1) * B] = Wb[k, stream]

    last_leg(y)
    for i in range(ny - 1):
        relay(block_of(i))
        if i >= 1:
            last_leg(block_of(i - 1))
            project(i - 1)
        if i % 2 == 1 and i // 2 + 1 <= reach:
            ring(i // 2 + 1)
            across(i // 2)
    last_leg(block_of(ny - 2))
    project(ny - 2)
    ring(reach)
    across(reach - 1)
    project(ny - 1)
    wait(Fr.at[pl.ds(0, ns - 1)], rV.at[0])
    loop(0, 8, toeplitz)
    across(reach)

    full = pad[HALO:]
    for side in range(2 if ny > 2 else 1):
        wait(Pe.at[0], rN.at[side])
        full = full + Pe[side]

    @pl.when(y > 0)
    def _():
        wait(Hr.at[pl.ds(0, ny - 1)], rH)

    @pl.when((y == 0) & (q > 0))
    def _():
        wait(Hr.at[pl.ds(0, ny)], rH)

    head = Hr[0].astype(F32)
    for k in range(1, ny):
        head = head + Hr[k].astype(F32)
    pad[HALO:] = full
    pad[:HALO] = head
    streams = []
    for stream in range(3):
        own = slice(stream * B, (stream + 1) * B)
        total = jnp.zeros((B, B), F32)
        for j in range(3):
            total = total + taps[stream, j:j + 1, :] * pad[HALO - j:HALO - j + B, own]
        streams.append(total)
    inner = streams[1] * streams[2]
    qi[0] = streams[0]
    qi[1] = inner

    turned = inner.T
    for k in range(cpd):
        Xs[:, k, :] = turned[k * ns:(k + 1) * ns]
    Xr[pl.ds(s, 1)] = Xs[pl.ds(s, 1)]
    loop(0, ns - 1, lambda k: send(Xs.at[away(k)], Xr.at[s], sV.at[1], rV.at[1], away(k), p))
    Xp[:ns] = jnp.zeros((ns, B), F32)

    wait(Xr.at[pl.ds(0, ns - 1)], rV.at[1])
    for ch in range(cpd):
        Xp[ns:] = Xr[:, ch, :]
        for d in range(ns):
            A[:, d * B:(d + 1) * B] = Xp[ns - d:2 * ns - d].astype(BF16)
        Ys[:, ch, :] = jnp.dot(A[...], T[ch], preferred_element_type=F32)
    Yr[pl.ds(s, 1)] = Ys[pl.ds(s, 1)]
    loop(0, ns - 1, lambda k: send(Ys.at[away(k)], Yr.at[s], sV.at[2], rV.at[2], away(k), p))
    wait(Yr.at[pl.ds(0, ns - 1)], rV.at[2])
    mix = jnp.concatenate([Yr[:, ch, :] for ch in range(cpd)], axis=0).T
    Gs[...] = (qi[0] * (mix + skip[...] * qi[1])).astype(BF16)

    gated = Gt.at[:, lanes(p)]
    for k in range(1, nzl):
        send(Gs, gated, sG, rG.at[nzl - k], s, ((zl + k) % nzl) * 2 + c)
    send(Gs, gated, sG, rG.at[0], s, mate)
    local(Gs, gated, loc.at[0])
    if nx > 2:
        wait(Wo.at[pl.ds(0, 2 * B)], rO.at[5])
    wait(Gs, loc.at[0])
    for k in sorted(range(1, nzl), key=lambda k: min(k, nzl - k)):
        other = Gt.at[:, lanes(((zl + k) % nzl) * 2 + c)]
        wait(Gs, rG.at[k])
        send(other, other, sG, rG.at[0], s, mate)
    wait(Gt.at[:, pl.ds(0, nzl * B)], rG.at[0])
    out[...] = jnp.dot(Gt[...], Wo[...], preferred_element_type=F32).astype(BF16)

    wait(F.at[pl.ds(0, ny - 1), :, pl.ds(0, B)], sF)
    wait(Wb.at[pl.ds(0, np_ - 1)], sW)
    if chain:
        @pl.when(end)
        def _():
            wait(F.at[:, :, pl.ds(0, 2 * B)], sZ)

        @pl.when(jnp.logical_not(end))
        def _():
            wait(F.at[:, :, pl.ds(0, 3 * B)], sZ)
            wait(F.at[:, :, pl.ds(0, B)], sE)
    else:
        wait(F.at[:, :, pl.ds(0, (nzl - 1) * B)], sZ)
    wait(F.at[:, :, pl.ds(0, nzl * B)], sC)
    for i in range(ny):
        tb = block_of(i)

        @pl.when((tb + 1 != y) & (halo_to(tb) < ns))
        def _(i=i):
            wait(Hr.at[0], sH.at[i])

        if distance(i) != 0:
            wait(Pe.at[0] if abs(distance(i)) == 1 else Ps.at[0], sP.at[i])

    for k in range(3):
        wait(Xs.at[pl.ds(0, ns - 1)], sV.at[k])
    wait(Gt.at[:, pl.ds(0, (2 * nzl - 1) * B)], sG)

    @pl.when(q != p)
    def _():
        wait(wout, sO.at[0])

    wait(wout, sO.at[1])
    wait(Wo.at[pl.ds(0, 2 * B), pl.ds(0, (ny - 1) * B)], sO.at[2])
    sides = Wo.at[pl.ds(0, 2 * B)]
    wait(sides, sO.at[3])
    if nx > 2:
        wait(sides, sO.at[4])
        wait(sides, sO.at[5])


def per_device(features, in_proj, short_taps, long_filter, skip_gain, out_proj):
    ns, np_ = lax.axis_size("seq"), lax.axis_size("tp")
    nx = np_ // 2
    ny = ns // np_
    cpd = B // ns
    dma = pltpu.SemaphoreType.DMA
    rows = pltpu.VMEM((ns, cpd, B), F32)
    return pl.pallas_call(
        functools.partial(kernel, ny, nx),
        out_shape=jax.ShapeDtypeStruct((B, ny * B), BF16),
        in_specs=[pl.BlockSpec(memory_space=pl.ANY)] * 6,
        out_specs=pl.BlockSpec(memory_space=pltpu.VMEM),
        scratch_shapes=[
            pltpu.VMEM((B, ny * B), BF16),
            pltpu.VMEM((3, B, B), BF16),
            pltpu.VMEM((3, 3, B), F32),
            pltpu.VMEM((B, B), F32),
            pltpu.VMEM((1, B), F32),
            pltpu.VMEM((B, B), BF16),
            pltpu.VMEM((ny, B, np_ * B), BF16),
            pltpu.VMEM((np_, 3, B, B), BF16),
            pltpu.VMEM((np_ * B, 3 * B), BF16),
            pltpu.VMEM((ny, B, 3 * B), BF16),
            pltpu.VMEM((ny, B, 3 * B), BF16),
            pltpu.VMEM((2, B, 3 * B), F32),
            pltpu.VMEM((2, B, 3 * B), F32),
            pltpu.VMEM((ny, HALO, 3 * B), BF16),
            pltpu.VMEM((ny, HALO, 3 * B), BF16),
            pltpu.VMEM((HALO + B, 3 * B), F32),
            pltpu.VMEM((2, B, B), F32),
            rows, rows, rows, rows, rows, rows,
            pltpu.VMEM((2 * ns, B), F32),
            pltpu.VMEM((ns, ns * B), BF16),
            pltpu.VMEM((cpd, ns * B, B), BF16),
            pltpu.VMEM((B, B), BF16),
            pltpu.VMEM((B, np_ * B), BF16),
            pltpu.VMEM((np_ * B, ny * B), BF16),
            dma((6,)), dma((3,)),
            dma, dma((ny,)),
            dma, dma((3,)),
            dma, dma((ny,)),
            dma, dma((ny,)),
            dma, dma((ny,)),
            dma((ny,)), dma((ny,)), dma((2,)),
            dma((ny,)), dma,
            dma((3,)), dma((3,)),
            dma, dma((max(2, np_ // 2),)),
            dma((6,)), dma((6,)), dma((ny,)), dma((ny,)), dma((ny,)), dma((ny,)),
            pltpu.SemaphoreType.REGULAR, pltpu.SemaphoreType.REGULAR,
        ],
        compiler_params=pltpu.CompilerParams(
            collective_id=0, has_side_effects=True
        ),
        name="operator",
    )(features, in_proj, short_taps, long_filter, skip_gain.reshape(1, B), out_proj)


def solution(mesh):
    return jax.shard_map(
        per_device,
        mesh=mesh,
        in_specs=(
            P("seq", "tp"),
            P(None, "seq", "tp"),
            P(None, None, "tp"),
            P("seq", "tp"),
            P("tp"),
            P("tp", "seq"),
        ),
        out_specs=P("seq", "tp"),
        check_vma=False,
    )
```
